32 devices in a mesh: gx: 4 (over x, core), gy: 8 (over z, y).
Axes of the slice: x: 2, y: 2, z: 4, core: 2. Of those that a mesh axis runs over, the one named last changes fastest.
Arguments:
- velocity: float32 [2, 11, 32, 1024], P(None, None, 'gx', 'gy'), may hold values from -6 to 6
- thickness: float32 [32, 1024], P('gx', 'gy'), may hold values from 0.5 to 2
- log_friction: float32 [32, 1024], P('gx', 'gy'), may hold values from -1 to 1
- obs_weight: float32 [32, 1024], P('gx', 'gy'), may hold values from 0.5 to 4
- ice_mask: int32 [32, 1024], P('gx', 'gy'), may hold values 0 or 1
- grounded: int32 [32, 1024], P('gx', 'gy'), may hold values 0 or 1
- probes: float32 [8, 32, 1024], P(None, 'gx', 'gy'), may hold values from -6 to 6
Outputs:
- hess_probe: float32 [8, 32, 1024], P(None, 'gx', 'gy')
The draws below stay inside these ranges and needn't reach their ends.
All inputs are finite; a program needn't handle non-finite values. No bound on the sum of `ice_mask` or of `grounded` on one device may be relied on, other than what follows from the above.
Results may differ from the reference program's by a relative error of at most 0.0003.
Values sent between devices are 32-bit elements; how exact they have to be, the bound alone decides.
A program may use at most 64 MiB of HBM per device.

```python
import math
import jax
import jax.numpy as jnp
from jax import lax

NL = 11
PROBES = 8
NX = 32
NY = 1024


def set_ends(values, key, least, largest):
    longest = values.shape.index(max(values.shape))
    spots = []
    for shift in (0, 1):
        where = [jax.random.randint(jax.random.fold_in(key, axis), (), 0, length) for axis, length in enumerate(values.shape)]
        where[longest] = (where[longest] + shift) % values.shape[longest]
        spots.append(tuple(where))
    return values.at[spots[0]].set(least).at[spots[1]].set(largest)


def level_of(rng, shape, shards, least, largest):
    loudness, own = 1.0, jax.random.fold_in(rng, 6)
    for dim, blocks in shards:
        steps = jnp.exp(jax.random.uniform(jax.random.fold_in(own, dim), (blocks,), jnp.float32, least / len(shards), largest / len(shards)))
        loudness = loudness * jnp.repeat(steps, shape[dim] // blocks).reshape([-1 if axis == dim else 1 for axis in range(len(shape))])
    return loudness


def centred(stream_key, dims, scale, limit, split=(), kind=jnp.bfloat16):
    drawn = jax.random.normal(stream_key, dims, jnp.float32) * scale
    if len(split) > 0:
        drawn = level_of(stream_key, dims, split, -0.22, 0.18) * drawn
    return jnp.clip(drawn, min=-limit, max=limit).astype(kind)


def setup_inputs(seed: int = 0) -> dict:
    key_list = jax.random.split(jax.random.key(seed), 8)
    return {
        "velocity": centred(key_list[0], (2, NL, NX, NY), 1.0, 6.0, ((2, 4), (3, 8)), jnp.float32),
        "thickness": jnp.clip(0.5 + 1.5 * jax.random.uniform(key_list[1], (NX, NY), jnp.float32) ** level_of(key_list[1], (NX, NY), ((0, 4), (1, 8)), -0.2, 0.2), 0.5, 2.0),
        "log_friction": jnp.clip(jax.random.uniform(key_list[2], (NX, NY), jnp.float32, -1.0, 1.0) * level_of(key_list[2], (NX, NY), ((0, 4), (1, 8)), -0.4, 0.0), -1.0, 1.0),
        "obs_weight": jnp.clip(jnp.exp(math.log(4.0) - 2.0794415 * jax.random.uniform(key_list[3], (NX, NY), jnp.float32) ** level_of(key_list[3], (NX, NY), ((0, 4), (1, 8)), -0.2, 0.2)), 0.5, 4.0),
        "ice_mask": set_ends((jax.random.randint(key_list[4], (NX, NY), 0, 4) < 3).astype(jnp.int32), jax.random.fold_in(key_list[4], 1), 0, 1),
        "grounded": set_ends((jax.random.randint(key_list[5], (NX, NY), 0, 3) < 2).astype(jnp.int32), jax.random.fold_in(key_list[5], 1), 0, 1),
        "probes": centred(key_list[6], (PROBES, NX, NY), 1.0, 6.0, ((1, 4), (2, 8)), jnp.float32),
    }


PRECISE = lax.Precision.HIGHEST
MASS_TERM = 0.1
STRAIN_OFFSET = 0.01

def viscosity(velocity_ext, thick_ext):
    layers = velocity_ext.shape[1]
    step_z = thick_ext[1:-1, 1:-1] / (layers - 1)
    speed_u = velocity_ext[0]
    speed_v = velocity_ext[1]
    grad_ux = 0.5 * (speed_u[:, 2:, 1:-1] - speed_u[:, :-2, 1:-1])
    grad_uy = 0.5 * (speed_u[:, 1:-1, 2:] - speed_u[:, 1:-1, :-2])
    grad_vx = 0.5 * (speed_v[:, 2:, 1:-1] - speed_v[:, :-2, 1:-1])
    grad_vy = 0.5 * (speed_v[:, 1:-1, 2:] - speed_v[:, 1:-1, :-2])
    middle = velocity_ext[:, :, 1:-1, 1:-1]
    column = jnp.concatenate([middle[:, :1], middle, middle[:, -1:]], axis=1)
    vertical_grad = (column[:, 2:] - column[:, :-2]) / (2.0 * step_z)
    strain = grad_ux * grad_ux + grad_vy * grad_vy + grad_ux * grad_vy + 0.25 * (grad_uy + grad_vx) ** 2 + 0.25 * (vertical_grad[0] ** 2 + vertical_grad[1] ** 2) + STRAIN_OFFSET
    return 0.5 * strain ** (-1.0 / 3.0)

def coefficients(visc_ext, mask_ext, thickness, grounded_f, log_friction):
    layers = visc_ext.shape[0]
    coef_x = 0.5 * (visc_ext[:, :-1, 1:-1] + visc_ext[:, 1:, 1:-1]) * (mask_ext[:-1, 1:-1] * mask_ext[1:, 1:-1])
    coef_y = 0.5 * (visc_ext[:, 1:-1, :-1] + visc_ext[:, 1:-1, 1:]) * (mask_ext[1:-1, :-1] * mask_ext[1:-1, 1:])
    interior = visc_ext[:, 1:-1, 1:-1]
    inverse_step = (layers - 1) / thickness
    coef_z = 0.5 * (interior[:-1] + interior[1:]) * (inverse_step * inverse_step)
    ice_own = mask_ext[1:-1, 1:-1]
    friction = ice_own * grounded_f * jnp.exp(log_friction)
    diag_base = MASS_TERM * ice_own + (1.0 - ice_own)
    zeros_upper = jnp.zeros((layers - 1,) + diag_base.shape, jnp.float32)
    diagonal = diag_base[None] + jnp.concatenate([friction[None], zeros_upper], axis=0)
    return (coef_x, coef_y, coef_z, diagonal, friction)

def anisotropy():
    aniso_x = jnp.array([4.0, 1.0], jnp.float32).reshape(2, 1, 1, 1)
    aniso_y = jnp.array([1.0, 4.0], jnp.float32).reshape(2, 1, 1, 1)
    return (aniso_x, aniso_y)

def operator_apply(extended, coef_x, coef_y, coef_z, diagonal):
    aniso_x, aniso_y = anisotropy()
    interior = extended[..., 1:-1, 1:-1]
    flux_x = coef_x * (extended[..., 1:, 1:-1] - extended[..., :-1, 1:-1])
    flux_y = coef_y * (extended[..., 1:-1, 1:] - extended[..., 1:-1, :-1])
    flux_z = coef_z * (interior[..., 1:, :, :] - interior[..., :-1, :, :])
    boundary_zero = jnp.zeros_like(flux_z[..., :1, :, :])
    vertical = jnp.concatenate([boundary_zero, flux_z], axis=-3) - jnp.concatenate([flux_z, boundary_zero], axis=-3)
    horizontal = aniso_x * (flux_x[..., :-1, :] - flux_x[..., 1:, :]) + aniso_y * (flux_y[..., :-1] - flux_y[..., 1:])
    return horizontal + vertical + diagonal * interior

def column_factors(coef_x, coef_y, coef_z, diagonal):
    aniso_x, aniso_y = anisotropy()
    layers = diagonal.shape[0]
    lateral = aniso_x * (coef_x[:, :-1] + coef_x[:, 1:]) + aniso_y * (coef_y[:, :, :-1] + coef_y[:, :, 1:])
    zero_layer = jnp.zeros_like(coef_z[:1])
    main_diag = lateral + diagonal + jnp.concatenate([zero_layer, coef_z], axis=0) + jnp.concatenate([coef_z, zero_layer], axis=0)
    ratios = []
    inverses = []
    for layer_index in range(layers):
        pivot_value = main_diag[:, layer_index]
        if layer_index > 0:
            pivot_value = pivot_value - coef_z[layer_index - 1] * ratios[-1]
        inverse = 1.0 / pivot_value
        inverses.append(inverse)
        if layer_index < layers - 1:
            ratios.append(coef_z[layer_index] * inverse)
    return (jnp.stack(ratios, axis=1), jnp.stack(inverses, axis=1))

def column_solve(residual, coef_z, ratios, inverses):
    layers = residual.shape[-3]
    forward_pass = []
    for layer_index in range(layers):
        current = residual[..., layer_index, :, :]
        if layer_index > 0:
            current = current + coef_z[layer_index - 1] * forward_pass[-1]
        forward_pass.append(current * inverses[:, layer_index])
    result = [forward_pass[-1]]
    for layer_index in range(layers - 2, -1, -1):
        result.append(forward_pass[layer_index] + ratios[:, layer_index] * result[-1])
    return jnp.stack(result[::-1], axis=-3)

def gram_matrix(left_block, right_block):
    probe_count = left_block.shape[0]
    return lax.dot_general(left_block.reshape(probe_count, -1), right_block.reshape(probe_count, -1), (((1,), (1,)), ((), ())), precision=PRECISE)

def combine(vectors, mixing):
    return jnp.tensordot(mixing, vectors, axes=((0,), (0,)), precision=PRECISE)

def small_solve(matrix, right_side):
    factor = jnp.linalg.cholesky(matrix)
    return jax.scipy.linalg.cho_solve((factor, True), right_side)

def block_solve(right_side, apply_fn, precond_fn):
    residual = right_side
    search = precond_fn(residual)
    norm_old = gram_matrix(residual, search)
    image = apply_fn(search)
    curvature = gram_matrix(search, image)
    step_mix = small_solve(curvature, norm_old)
    solution = combine(search, step_mix)
    residual = residual - combine(image, step_mix)
    precon = precond_fn(residual)
    norm_new = gram_matrix(residual, precon)
    update_mix = small_solve(norm_old, norm_new)
    search = precon + combine(search, update_mix)
    image = apply_fn(search)
    curvature = gram_matrix(search, image)
    step_mix = small_solve(curvature, norm_new)
    return solution + combine(search, step_mix)

def reference(velocity, thickness, log_friction, obs_weight, ice_mask, grounded, probes):
    layers = velocity.shape[1]
    mask_f = ice_mask.astype(jnp.float32)
    grounded_f = grounded.astype(jnp.float32)
    velocity_ext = jnp.pad(velocity, ((0, 0), (0, 0), (1, 1), (1, 1)))
    thick_ext = jnp.pad(thickness, 1, mode='edge')
    visc_node = viscosity(velocity_ext, thick_ext)
    visc_ext = jnp.pad(jnp.where(mask_f[None] > 0.5, visc_node, 0.0), ((0, 0), (1, 1), (1, 1)))
    mask_ext = jnp.pad(mask_f, 1)
    coef_x, coef_y, coef_z, diagonal, friction = coefficients(visc_ext, mask_ext, thickness, grounded_f, log_friction)
    ratios, inverses = column_factors(coef_x, coef_y, coef_z, diagonal)

    def apply_one(single):
        return operator_apply(jnp.pad(single, ((0, 0), (0, 0), (1, 1), (1, 1))), coef_x, coef_y, coef_z, diagonal)

    def apply_all(vectors):
        return lax.map(apply_one, vectors)

    def precond_all(vectors):
        return lax.map(lambda single: column_solve(single, coef_z, ratios, inverses), vectors)
    probe_count = probes.shape[0]
    upper_zero = jnp.zeros((probe_count, 2, layers - 1) + thickness.shape, jnp.float32)
    bottom = (friction[None] * probes)[:, None] * velocity[None, :, 0]
    forward_rhs = jnp.concatenate([bottom[:, :, None], upper_zero], axis=2)
    delta_u = block_solve(forward_rhs, apply_all, precond_all)
    surface = (obs_weight * mask_f)[None, None] * delta_u[:, :, layers - 1]
    adjoint_rhs = jnp.concatenate([upper_zero, surface[:, :, None]], axis=2)
    delta_lam = block_solve(adjoint_rhs, apply_all, precond_all)
    return friction[None] * jnp.sum(velocity[None, :, 0] * delta_lam[:, :, 0], axis=1)
```

```python
import functools

import jax
import jax.numpy as jnp
from jax import lax
from jax.experimental import pallas as pl
from jax.experimental.pallas import tpu as pltpu
from jax.sharding import PartitionSpec as P

MASS_TERM = 0.1
STRAIN_OFFSET = 0.01
ANISO_X = (4.0, 1.0)
ANISO_Y = (1.0, 4.0)
HIGHEST = lax.Precision.HIGHEST
MESH = pl.DeviceIdType.MESH
PAIR = 2


def round_up(value, step):
    return (value + step - 1) // step * step


def kernel(
    sizes,
    vel_ref, thick_ref, logf_ref, obs_ref, ice_ref, ground_ref, probes_ref,
    out_ref,
    xs1, xr1, ys1, yr1,
    xs2, xr2, ys2, yr2,
    xs3, xr3, ys3, yr3,
    ys4, yr4, ub,
    coef, kzs, ratio, inverse, green, weight, bext, bedge, uedge,
    fields, tile_src, landed,
    send_sem, recv_sem, ar_send, ar_recv,
):
    n_gx, n_gy = sizes
    layers = vel_ref.shape[1]
    rows = vel_ref.shape[2]
    lanes = vel_ref.shape[3]
    probes = probes_ref.shape[0]
    half = probes // 2
    comps = 2 * layers
    last = layers - 1
    ix = lax.axis_index("gx")
    iy = lax.axis_index("gy")
    tile = (rows, lanes)
    lane = lax.broadcasted_iota(jnp.int32, tile, 1)
    sub = lax.broadcasted_iota(jnp.int32, tile, 0)
    slot = ((lane + 1) >> 1) & (lanes // 2 - 1)
    even = (lane & 1) == 0
    lane_first = lane == 0
    lane_last = lane == lanes - 1
    sub_first = sub == 0
    sub_last = sub == rows - 1

    sent = []
    barrier = pltpu.get_barrier_semaphore()
    peers = [
        {"gx": lax.rem(ix + step // n_gy, n_gx), "gy": lax.rem(iy + step % n_gy, n_gy)} for step in range(1, n_gx * n_gy)
    ]
    for peer in peers:
        pl.semaphore_signal(barrier, inc=1, device_id=peer, device_id_type=MESH)

    def transfer(phase, way, src, dst):
        axis, idx, count = ("gx", ix, n_gx) if way < 2 else ("gy", iy, n_gy)
        down = way % 2 == 0
        has_dst = idx > 0 if down else idx < count - 1
        has_src = idx < count - 1 if down else idx > 0
        copy = pltpu.make_async_remote_copy(
            src_ref=src, dst_ref=dst,
            send_sem=send_sem.at[phase, way], recv_sem=recv_sem.at[phase, way],
            device_id={axis: idx - 1 if down else idx + 1}, device_id_type=MESH,
        )
        return copy, dst, has_dst, has_src

    def exchange(phase, x_src, x_dst, y_src, y_dst):
        return (
            transfer(phase, 0, x_src[0], x_dst[1]),
            transfer(phase, 1, x_src[1], x_dst[0]),
            transfer(phase, 2, y_src, y_dst[1]),
            transfer(phase, 3, y_src, y_dst[0]),
        )

    def clear(transfers):
        for _, dst, _, has_src in transfers:
            @pl.when(jnp.logical_not(has_src))
            def _(dst=dst):
                dst[...] = jnp.zeros(dst.shape, jnp.float32)

    def start(transfers):
        for copy, _, has_dst, _ in transfers:
            pl.when(has_dst)(copy.start)

    def finish(transfers):
        for copy, _, has_dst, has_src in transfers:
            pl.when(has_src)(copy.wait_recv)
        sent.extend((copy, has_dst) for copy, _, has_dst, _ in transfers)

    ex1 = exchange(0, (xs1.at[0], xs1.at[1]), (xr1.at[0], xr1.at[1]), ys1, (yr1.at[0], yr1.at[1]))
    ex2 = exchange(1, (xs2.at[0], xs2.at[1]), (xr2.at[0], xr2.at[1]), ys2, (yr2.at[0], yr2.at[1]))
    ex3 = exchange(2, (xs3.at[0], xs3.at[1]), (xr3.at[0], xr3.at[1]), ys3, (yr3.at[0], yr3.at[1]))
    pairs_of_rows = rows // PAIR
    ex_rows = [
        (transfer(3 + p, 0, ub.at[p, 1], ub.at[p, rows + 1]), transfer(3 + p, 1, ub.at[p, rows], ub.at[p, 0]))
        for p in range(2)
    ]
    ex_packs = [
        [
            tuple(
                transfer(
                    3 + p + 2 * t, 2 + w, ys4.at[p, pl.ds(t * probes, probes)],
                    yr4.at[p, 1 - w, pl.ds(t * probes, probes)],
                )
                for w in range(2)
            )
            for t in range(pairs_of_rows)
        ]
        for p in range(2)
    ]

    def pack(tiles):
        packed = tiles[0]
        for m in range(1, len(tiles)):
            packed = jnp.where(slot == m, pltpu.roll(tiles[m], 2 * m, 1), packed)
        return packed

    def merge(south, north):
        return jnp.where(even, pltpu.roll(south, 1, 1), pltpu.roll(north, lanes - 1, 1))

    def unpack(merged, m):
        return merged if m == 0 else pltpu.roll(merged, lanes - 2 * m, 1)

    def west(t, row):
        return jnp.where(sub_first, row, pltpu.roll(t, 1, 0))

    def east(t, row):
        return jnp.where(sub_last, row, pltpu.roll(t, rows - 1, 0))

    def south(t, edge):
        return jnp.where(lane_first, edge, pltpu.roll(t, 1, 1))

    def north(t, edge):
        return jnp.where(lane_last, edge, pltpu.roll(t, lanes - 1, 1))

    def ahead(t, d):
        return t if d == 0 else pltpu.roll(t, probes - d, 0)

    mask = ice_ref[...].astype(jnp.float32)
    friction = mask * ground_ref[...].astype(jnp.float32) * jnp.exp(logf_ref[...])
    wm = obs_ref[...] * mask
    fields[0] = friction
    fields[1] = wm
    natural = [vel_ref[c, l] for c in range(2) for l in range(layers)] + [mask, wm]
    for k, t in enumerate(natural):
        xs1[0, k : k + 1, :] = t[0:1, :]
        xs1[1, k : k + 1, :] = t[rows - 1 : rows, :]
    base1 = round_up(len(natural), 8)
    drive = [friction * vel_ref[c, 0] for c in range(2)]
    for i in range(rows):
        probe = probes_ref[:, i, :]
        for c in range(2):
            bext[0, c, i + 1] = probe * drive[c][i : i + 1, :]
    for c in range(2):
        xs1[0, base1 + c * probes : base1 + (c + 1) * probes, :] = bext[0, c, 1]
        xs1[1, base1 + c * probes : base1 + (c + 1) * probes, :] = bext[0, c, rows]
    ys1[0:rows, :] = pack(natural)
    ys1[rows:, :] = pack([bext[0, c, i + 1] for c in range(2) for i in range(rows)])

    for ex in [ex1, ex2, ex3] + ex_rows + ex_packs[0] + ex_packs[1]:
        clear(ex)
    pl.semaphore_wait(barrier, len(peers))
    start(ex1)
    finish(ex1)

    merged1 = merge(yr1[0, 0:rows, :], yr1[1, 0:rows, :])
    edge1 = [unpack(merged1, k) for k in range(len(natural))]
    mergedb = merge(yr1[0, rows:, :], yr1[1, rows:, :])
    for c in range(2):
        bext[0, c, 0] = xr1[0, base1 + c * probes : base1 + (c + 1) * probes, :]
        bext[0, c, rows + 1] = xr1[1, base1 + c * probes : base1 + (c + 1) * probes, :]
        for i in range(rows):
            bedge[0, c, i] = unpack(mergedb, c * rows + i)

    def around(t, k):
        return (
            west(t, xr1[0, k : k + 1, :]), east(t, xr1[1, k : k + 1, :]),
            south(t, edge1[k]), north(t, edge1[k]),
        )

    inverse_step = last / thick_ref[...]
    half_step = 0.5 * inverse_step
    visc = []
    for l in range(layers):
        grads = []
        for c in range(2):
            w, e, s, n = around(vel_ref[c, l], c * layers + l)
            dz = (vel_ref[c, min(l + 1, last)] - vel_ref[c, max(l - 1, 0)]) * half_step
            grads.append((0.5 * (e - w), 0.5 * (n - s), dz))
        (ux, uy, uz), (vx, vy, vz) = grads
        shear = uy + vx
        strain = ux * ux + vy * vy + ux * vy + 0.25 * (shear * shear) + 0.25 * (uz * uz + vz * vz) + STRAIN_OFFSET
        root = jnp.exp(jnp.log(strain) * (-1.0 / 3.0))
        root = root + root * (1.0 - strain * root * root * root) * (1.0 / 3.0)
        mu = jnp.where(mask > 0.5, 0.5 * root, 0.0)
        visc.append(mu)
        xs2[0, l : l + 1, :] = mu[0:1, :]
        xs2[1, l : l + 1, :] = mu[rows - 1 : rows, :]
    ys2[...] = pack(visc)
    start(ex2)
    mask_w, mask_e, mask_s, mask_n = (0.5 * mask * m for m in around(mask, comps))
    step2 = inverse_step * inverse_step
    kz = [0.5 * (visc[l] + visc[l + 1]) * step2 for l in range(last)]
    for l in range(last):
        kzs[l] = kz[l]
    diag = MASS_TERM * mask + (1.0 - mask)
    finish(ex2)
    merged2 = merge(yr2[0], yr2[1])
    for l in range(layers):
        mu = visc[l]
        edge = unpack(merged2, l)
        coef[0, l] = (mu + west(mu, xr2[0, l : l + 1, :])) * mask_w
        coef[1, l] = (mu + east(mu, xr2[1, l : l + 1, :])) * mask_e
        coef[2, l] = (mu + south(mu, edge)) * mask_s
        coef[3, l] = (mu + north(mu, edge)) * mask_n

    for c in range(2):
        ratios, inverses = [], []
        for l in range(layers):
            pivot = ANISO_X[c] * (coef[0, l] + coef[1, l]) + ANISO_Y[c] * (coef[2, l] + coef[3, l]) + diag
            if l == 0:
                pivot = pivot + friction
            if l > 0:
                pivot = pivot + kz[l - 1]
            if l < last:
                pivot = pivot + kz[l]
            if l > 0:
                pivot = pivot - kz[l - 1] * ratios[-1]
            inv = 1.0 / pivot
            inverses.append(inv)
            inverse[c, l] = inv
            if l < last:
                ratios.append(kz[l] * inv)
                ratio[c, l] = ratios[-1]
        up = [inverses[0]]
        for l in range(1, layers):
            up.append(kz[l - 1] * up[-1] * inverses[l])
        low, top = up[last], inverses[last]
        for l in range(last, -1, -1):
            if l < last:
                low = up[l] + ratios[l] * low
                top = ratios[l] * top
            green[0, c, l] = low
            green[1, c, l] = top
    tiles3 = []
    for p in range(2):
        for c in range(2):
            for l in range(layers):
                k = len(tiles3)
                t = green[p, c, l]
                tiles3.append(t)
                xs3[0, k : k + 1, :] = t[0:1, :]
                xs3[1, k : k + 1, :] = t[rows - 1 : rows, :]
    ys3[...] = pack(tiles3)
    start(ex3)
    finish(ex3)
    merged3 = merge(yr3[0], yr3[1])
    for p in range(2):
        for c in range(2):
            for l in range(layers):
                k = (p * 2 + c) * layers + l
                t = green[p, c, l]
                edge = unpack(merged3, k)
                weight[p, c, 0, l] = ANISO_X[c] * coef[0, l] * west(t, xr3[0, k : k + 1, :])
                weight[p, c, 1, l] = ANISO_X[c] * coef[1, l] * east(t, xr3[1, k : k + 1, :])
                weight[p, c, 2, l] = ANISO_Y[c] * coef[2, l] * south(t, edge)
                weight[p, c, 3, l] = ANISO_Y[c] * coef[3, l] * north(t, edge)

    zero = jnp.zeros((probes, lanes), jnp.float32)

    def outer(acc, left, right):
        return tuple(acc[d] + left * ahead(right, d) for d in range(half + 1))

    def place(grams, g, acc):
        for d in range(half + 1):
            total = jnp.broadcast_to(jnp.sum(acc[d], axis=1, keepdims=True), (probes, lanes))
            grams = jnp.where(lane == g * probes + (sub + d) % probes, total, grams)
            if 0 < d < half:
                moved = pltpu.roll(total, d, 0)
                grams = jnp.where(lane == g * probes + (sub + probes - d) % probes, moved, grams)
        return grams

    def solve(p):
        src = 0 if p == 0 else last
        dst = last - src

        def first(t, accs):
            acc_s, acc_1, acc_2 = accs
            packed = None
            for ii in range(PAIR):
                i = t * PAIR + ii
                for c in range(2):
                    b0 = bext[p, c, i + 1]
                    bw = bext[p, c, i]
                    be = bext[p, c, i + 2]
                    edge = bedge[p, c, i]
                    bs = south(b0, edge)
                    bn = north(b0, edge)
                    lateral, y = [], []
                    for l in range(layers):
                        n1 = (
                            weight[p, c, 0, l, pl.ds(i, 1), :] * bw
                            + weight[p, c, 1, l, pl.ds(i, 1), :] * be
                            + weight[p, c, 2, l, pl.ds(i, 1), :] * bs
                            + weight[p, c, 3, l, pl.ds(i, 1), :] * bn
                        )
                        lateral.append(n1)
                        if l > 0:
                            n1 = n1 + kzs[l - 1, pl.ds(i, 1), :] * y[-1]
                        y.append(n1 * inverse[c, l, pl.ds(i, 1), :])
                    x = y[last]
                    for l in range(last, -1, -1):
                        if l < last:
                            x = y[l] + ratio[c, l, pl.ds(i, 1), :] * x
                        ub[p, i + 1, c * layers + l] = x
                        m = (ii * 2 + c) * layers + l
                        moved = x if m == 0 else pltpu.roll(x, 2 * m, 1)
                        packed = moved if packed is None else jnp.where(slot == m, moved, packed)
                        acc_2 = outer(acc_2, lateral[l], x)
                        if l == src:
                            acc_1 = outer(acc_1, b0, x)
                    acc_s = outer(acc_s, green[p, c, src, pl.ds(i, 1), :] * b0, b0)
            ys4[p, pl.ds(t * probes, probes), :] = packed
            return acc_s, acc_1, acc_2

        none = (zero,) * (half + 1)
        accs = (none, none, none)
        order = [0, pairs_of_rows - 1] + list(range(1, pairs_of_rows - 1))
        for n, t in enumerate(order):
            accs = first(t, accs)
            start(ex_packs[p][t])
            if n == 1:
                start(ex_rows[p])
        grams = jnp.zeros((probes, lanes), jnp.float32)
        for g in range(3):
            grams = place(grams, g, accs[g])
        for t in order:
            finish(ex_packs[p][t])
        finish(ex_rows[p])

        def second(t, acc_3):
            at = pl.ds(pl.multiple_of(t * probes, probes), probes)
            merged = merge(yr4[p, 0, at, :], yr4[p, 1, at, :])
            for ii in range(PAIR):
                i = t * PAIR + ii
                for l in range(layers):
                    cw, ce, cs, cn = (coef[q, l, pl.ds(i, 1), :] for q in range(4))
                    for c in range(2):
                        k = c * layers + l
                        w0 = ub[p, i + 1, k]
                        edge = unpack(merged, ii * comps + k)
                        if l == dst:
                            uedge[c, i] = edge
                        n2 = ANISO_X[c] * (cw * ub[p, i, k] + ce * ub[p, i + 2, k]) + ANISO_Y[c] * (
                            cs * south(w0, edge) + cn * north(w0, edge)
                        )
                        acc_3 = outer(acc_3, n2, w0)
            return acc_3

        acc_3 = lax.fori_loop(0, rows // PAIR, second, none)

        grams = place(grams, 3, acc_3)

        width = 4 * probes
        packed = grams
        for q in range(1, probes // PAIR):
            packed = jnp.where(lane < q * width, packed, pltpu.roll(pltpu.roll(grams, probes - PAIR * q, 0), q * width, 1))
        own = pl.ds((ix * n_gy + iy) * PAIR, PAIR)
        landed[p, own, :] = packed[0:PAIR, :]
        total_rows = pl.ds(0, PAIR * len(peers))
        tile_src[p] = packed[0:PAIR, :]
        for peer in peers:
            pltpu.make_async_remote_copy(
                src_ref=tile_src.at[p], dst_ref=landed.at[p, own], send_sem=ar_send.at[p], recv_sem=ar_recv.at[p],
                device_id=peer, device_id_type=MESH,
            ).start()
        everyone = pltpu.make_async_remote_copy(
            src_ref=landed.at[p, total_rows], dst_ref=landed.at[p, total_rows], send_sem=ar_send.at[p],
            recv_sem=ar_recv.at[p], device_id=peers[0], device_id_type=MESH,
        )
        everyone.wait_recv()
        sent.append((everyone, None))
        parts = [landed[p, k * probes : (k + 1) * probes, :] for k in range(landed.shape[1] // probes)]
        while len(parts) > 1:
            parts = [parts[k] + parts[k + 1] if k + 1 < len(parts) else parts[k] for k in range(0, len(parts), 2)]
        packed = parts[0]
        shift = PAIR
        while shift < probes:
            packed = packed + pltpu.roll(packed, shift, 0)
            shift *= 2
        grams = packed
        for q in range(1, probes // PAIR):
            grams = jnp.where(sub < PAIR * q, grams, pltpu.roll(packed, lanes - q * width, 1))

        diff = grams - pltpu.roll(grams, lanes - probes, 1)
        upper = jnp.where(lane < 2 * probes, diff, pltpu.roll(grams, 2 * probes, 1))
        lower = jnp.where(lane < 2 * probes, pltpu.roll(diff, lanes - probes, 1), pltpu.roll(grams, probes, 1))
        size = 2 * probes
        both = [upper, lower]
        scale = [jnp.sum(jnp.where(lane == sub + h * probes, both[h], 0.0), axis=1, keepdims=True) for h in range(2)]
        for k in range(size):
            h, r = k // probes, k % probes
            row = both[h][r : r + 1, :]
            pivot = row[:, k : k + 1]
            inv = jnp.where(pivot > 1e-6 * scale[h][r : r + 1, :], 1.0 / pivot, 0.0)
            row = row * inv
            for q in range(2):
                updated = both[q] - both[q][:, k : k + 1] * row
                both[q] = jnp.where(sub == r, row, updated) if q == h else updated
        pick = (lane == sub + size).astype(jnp.float32)
        return lax.dot_general(
            pick, jnp.concatenate(both, axis=0), (((1,), (1,)), ((), ())),
            precision=HIGHEST, preferred_element_type=jnp.float32,
        )

    def mix(mixing, pairs):
        stacked = jnp.concatenate([jnp.concatenate(pair, axis=0) for pair in pairs], axis=1)
        mixed = lax.dot_general(
            mixing, stacked, (((1,), (0,)), ((), ())), precision=HIGHEST, preferred_element_type=jnp.float32
        )
        return [mixed[:, k * lanes : (k + 1) * lanes] for k in range(len(pairs))]

    mixing = solve(0)
    wm_edge = edge1[comps + 1]
    for c in range(2):
        k = c * layers + last
        inner = green[0, c, last]
        edge = unpack(merged3, k)
        pairs = [(xr3[0, k : k + 1, :] * bext[0, c, 0], ub[0, 0, k])]
        pairs += [(inner[i : i + 1, :] * bext[0, c, i + 1], ub[0, i + 1, k]) for i in range(rows)]
        pairs += [(xr3[1, k : k + 1, :] * bext[0, c, rows + 1], ub[0, rows + 1, k])]
        pairs += [(edge[i : i + 1, :] * bedge[0, c, i], uedge[c, i]) for i in range(rows)]
        mixed = mix(mixing, pairs)
        bext[1, c, 0] = mixed[0] * xr1[0, comps + 1 : comps + 2, :]
        bext[1, c, rows + 1] = mixed[rows + 1] * xr1[1, comps + 1 : comps + 2, :]
        for i in range(rows):
            bext[1, c, i + 1] = mixed[i + 1] * wm[i : i + 1, :]
            bedge[1, c, i] = mixed[rows + 2 + i] * wm_edge[i : i + 1, :]

    mixing = solve(1)
    results = []
    for c in range(2):
        inner = green[1, c, 0]
        results.append(mix(mixing, [
            (inner[i : i + 1, :] * bext[1, c, i + 1], ub[1, i + 1, c * layers]) for i in range(rows)
        ]))
    for i in range(rows):
        out_ref[:, i, :] = drive[0][i : i + 1, :] * results[0][i] + drive[1][i : i + 1, :] * results[1][i]
    for copy, has_dst in sent:
        if has_dst is None:
            copy.wait_send()
        else:
            pl.when(has_dst)(copy.wait_send)


def body(sizes, velocity, thickness, log_friction, obs_weight, ice_mask, grounded, probes):
    layers, rows, lanes = velocity.shape[1:]
    count = probes.shape[0]
    comps = 2 * layers
    n_gx, n_gy = sizes
    rows1 = round_up(comps + 2, 8) + 2 * count
    rows2 = round_up(layers, 8)
    rows3 = round_up(2 * comps, 8)
    packs = rows // PAIR * count

    def vmem(*shape):
        return pltpu.VMEM(shape, jnp.float32)

    def borders(x_rows, y_rows):
        return [vmem(2, x_rows, lanes), vmem(2, x_rows, lanes), vmem(y_rows, lanes), vmem(2, y_rows, lanes)]

    sem = pltpu.SemaphoreType.DMA
    scratch = (
        borders(rows1, rows + count)
        + borders(rows2, rows)
        + borders(rows3, rows)
        + [vmem(2, packs, lanes), vmem(2, 2, packs, lanes), vmem(2, rows + 2, comps, count, lanes)]
        + [
            vmem(4, layers, rows, lanes), vmem(layers - 1, rows, lanes),
            vmem(2, layers - 1, rows, lanes), vmem(2, layers, rows, lanes),
            vmem(2, 2, layers, rows, lanes), vmem(2, 2, 4, layers, rows, lanes),
            vmem(2, 2, rows + 2, count, lanes), vmem(2, 2, rows, count, lanes), vmem(2, rows, count, lanes),
            vmem(2, rows, lanes), vmem(2, PAIR, lanes), vmem(2, PAIR * n_gx * n_gy, lanes),
        ]
        + [sem((3 + 2 * (rows // PAIR), 4)), sem((3 + 2 * (rows // PAIR), 4)), sem((2,)), sem((2,))]
    )
    return pl.pallas_call(
        functools.partial(kernel, sizes),
        out_shape=jax.ShapeDtypeStruct(probes.shape, jnp.float32),
        in_specs=[pl.BlockSpec(memory_space=pltpu.VMEM)] * 7,
        out_specs=pl.BlockSpec(memory_space=pltpu.VMEM),
        scratch_shapes=scratch,
        compiler_params=pltpu.CompilerParams(collective_id=0, has_side_effects=True),
        name="hessian_probe",
    )(velocity, thickness, log_friction, obs_weight, ice_mask, grounded, probes)


def solution(mesh):
    sizes = (mesh.shape["gx"], mesh.shape["gy"])
    in_specs = (
        P(None, None, "gx", "gy"),
        P("gx", "gy"),
        P("gx", "gy"),
        P("gx", "gy"),
        P("gx", "gy"),
        P("gx", "gy"),
        P(None, "gx", "gy"),
    )
    out_specs = P(None, "gx", "gy")
    return jax.shard_map(
        functools.partial(body, sizes), mesh=mesh, in_specs=in_specs, out_specs=out_specs, check_vma=False
    )
```

```python
import functools

import jax
import jax.numpy as jnp
from jax import lax
from jax.experimental import pallas as pl
from jax.experimental.pallas import tpu as pltpu
from jax.sharding import PartitionSpec as P

MASS_TERM = 0.1
STRAIN_OFFSET = 0.01
ANISO_X = (4.0, 1.0)
ANISO_Y = (1.0, 4.0)
HIGHEST = lax.Precision.HIGHEST
MESH = pl.DeviceIdType.MESH
PAIR = 2
REACH = 5
SLOT = 2 * REACH
WEST, EAST, SOUTH, NORTH = range(4)
DIRS = range(4)
FORMS = 4


class Field:
    def __init__(self, tiles):
        self.tiles = tiles

    def _with(self, other, op):
        if isinstance(other, Field):
            return Field([None if a is None or b is None else op(a, b) for a, b in zip(self.tiles, other.tiles)])
        return Field([None if a is None else op(a, other) for a in self.tiles])

    def __add__(self, other):
        return self._with(other, lambda a, b: a + b)

    def __sub__(self, other):
        return self._with(other, lambda a, b: a - b)

    def __mul__(self, other):
        return self._with(other, lambda a, b: a * b)

    __radd__ = __add__
    __rmul__ = __mul__

    def map(self, op):
        return Field([None if a is None else op(a) for a in self.tiles])


def kernel(
    sizes,
    vel_ref, thick_ref, logf_ref, obs_ref, ice_ref, ground_ref, probes_ref,
    out_ref,
    row, hrow, tn, ts, edge_src, edge_dst,
    coef, kzs, ratio, inverse, green, wsc, hsc, hshift, quad, drv, wmx, probe_strip,
    bx, left, right, basis, results, tile_src, landed,
    send_sem, recv_sem, ar_send, ar_recv,
):
    n_gx, n_gy = sizes
    layers = vel_ref.shape[1]
    rows = vel_ref.shape[2]
    lanes = vel_ref.shape[3]
    probes = probes_ref.shape[0]
    last = layers - 1
    half = rows // 2
    per_tile = layers + 1
    n_fields = 2 * per_tile + probes + 2
    ix = lax.axis_index("gx")
    iy = lax.axis_index("gy")
    tile = (rows, lanes)
    lane = lax.broadcasted_iota(jnp.int32, tile, 1)
    sub = lax.broadcasted_iota(jnp.int32, tile, 0)
    lane_first = lane == 0
    lane_last = lane == lanes - 1
    sub_first = sub == 0
    sub_last = sub == rows - 1
    slot_id = lane // SLOT
    high = lane - slot_id * SLOT < REACH

    barrier = pltpu.get_barrier_semaphore()
    peers = [
        {"gx": lax.rem(ix + step // n_gy, n_gx), "gy": lax.rem(iy + step % n_gy, n_gy)} for step in range(1, n_gx * n_gy)
    ]
    for peer in peers:
        pl.semaphore_signal(barrier, inc=1, device_id=peer, device_id_type=MESH)

    def lane_roll(t, shift):
        shift = shift % lanes
        return t if shift == 0 else pltpu.roll(t, shift, 1)

    def sub_roll(t, shift):
        return pltpu.roll(t, shift % rows, 0)

    def inside(dx, dy):
        tests = []
        if dx:
            tests.append(ix > 0 if dx < 0 else ix < n_gx - 1)
        if dy:
            tests.append(iy > 0 if dy < 0 else iy < n_gy - 1)
        return functools.reduce(jnp.logical_and, tests)

    def transfer(k, dx, dy, src, dst):
        target = {}
        if dx:
            target["gx"] = ix + dx
        if dy:
            target["gy"] = iy + dy
        copy = pltpu.make_async_remote_copy(
            src_ref=src, dst_ref=dst, send_sem=send_sem.at[k], recv_sem=recv_sem.at[k],
            device_id=target, device_id_type=MESH,
        )
        return copy, dst, inside(dx, dy), inside(-dx, -dy)

    low, top = pl.ds(0, half), pl.ds(half, half)
    corner_low, corner_top = pl.ds(rows, half), pl.ds(rows + half, half)
    own_pack = pl.ds(n_fields, 3)
    whole = pl.ds(0, rows)
    everything = pl.ds(0, n_fields + 3)
    packs = pl.ds(0, 3)
    exchange = [
        transfer(0, -1, 0, row.at[everything, low], hrow.at[everything, low]),
        transfer(1, 1, 0, row.at[everything, top], hrow.at[everything, top]),
        transfer(2, 0, -1, row.at[own_pack, whole], tn.at[packs, whole]),
        transfer(3, 0, 1, row.at[own_pack, whole], ts.at[packs, whole]),
        transfer(4, -1, -1, row.at[own_pack, low], tn.at[packs, corner_low]),
        transfer(5, 1, -1, row.at[own_pack, top], tn.at[packs, corner_top]),
        transfer(6, -1, 1, row.at[own_pack, low], ts.at[packs, corner_low]),
        transfer(7, 1, 1, row.at[own_pack, top], ts.at[packs, corner_top]),
    ]
    edge_copy = transfer(8, -1, 0, edge_src, edge_dst)

    mask_own = ice_ref[...].astype(jnp.float32)
    friction_own = mask_own * ground_ref[...].astype(jnp.float32) * jnp.exp(logf_ref[...])
    wm_own = obs_ref[...] * mask_own
    own = [vel_ref[0, l] for l in range(layers)] + [thick_ref[...]]
    own += [vel_ref[1, l] for l in range(layers)] + [mask_own]
    own += [probes_ref[p] for p in range(probes)] + [friction_own, wm_own]
    for f, t in enumerate(own):
        row[f] = t
    for k in range(3):
        packed = None
        for s, t in enumerate(own[k * per_tile : (k + 1) * per_tile]):
            moved = lane_roll(t, s * SLOT + REACH)
            packed = moved if packed is None else jnp.where(slot_id == s, moved, packed)
        row[n_fields + k] = packed

    for _, dst, _, has_src in exchange + [edge_copy]:
        @pl.when(jnp.logical_not(has_src))
        def _(dst=dst):
            dst[...] = jnp.zeros(dst.shape, jnp.float32)
    pl.semaphore_wait(barrier, len(peers))
    for copy, _, has_dst, _ in exchange:
        pl.when(has_dst)(copy.start)
    for copy, _, _, has_src in exchange:
        pl.when(has_src)(copy.wait_recv)

    def shifted(f, axis, forward):
        if axis == 0:
            at, move, pairs = (sub_first, -1, ((0, 1), (1, 0), (2, 3), (3, 2))) if forward else (sub_last, 1, ((0, 1), (1, 0), (2, 3), (3, 2)))
            roll = sub_roll
        else:
            at, move, pairs = (lane_first, -1, ((0, 2), (1, 3), (2, 0), (3, 1))) if forward else (lane_last, 1, ((0, 2), (1, 3), (2, 0), (3, 1)))
            roll = lane_roll
        tiles = [None] * 4
        for a, b in pairs:
            if f.tiles[a] is not None and f.tiles[b] is not None:
                tiles[a] = roll(jnp.where(at, f.tiles[b], f.tiles[a]), move)
        return Field(tiles)

    def neighbour(f, d):
        return shifted(f, 0 if d in (WEST, EAST) else 1, d in (EAST, NORTH))

    both_packs = [
        [jnp.where(high, ts[k, pl.ds(h * rows, rows), :], tn[k, pl.ds(h * rows, rows), :]) for h in range(2)]
        for k in range(3)
    ]

    def strip(packs_of, s):
        return [lane_roll(t, -(s * SLOT + REACH)) for t in packs_of]

    def assemble(f):
        return Field([own[f], hrow[f]] + strip(both_packs[f // per_tile], f % per_tile))

    thick = assemble(layers).map(lambda t: jnp.where(t > 0.0, t, 1.0))
    inverse_step = thick.map(lambda t: last / t)
    mask = assemble(per_tile + layers)
    friction = assemble(2 * per_tile + probes)
    wm = assemble(2 * per_tile + probes + 1)

    def viscosity(ux, uy, uz, vx, vy, vz):
        shear = uy + vx
        strain = ux * ux + vy * vy + ux * vy + 0.25 * (shear * shear) + 0.25 * (uz * uz + vz * vz) + STRAIN_OFFSET
        root = jnp.exp(jnp.log(strain) * (-1.0 / 3.0))
        root = root + root * (1.0 - strain * root * root * root) * (1.0 / 3.0)
        return 0.5 * root

    strips = []
    for north_side in (True, False):
        def side(k):
            tiles = []
            for h in range(2):
                mine = row[n_fields + k] if h == 0 else hrow[n_fields + k]
                theirs = (tn if north_side else ts)[k, pl.ds(h * rows, rows), :]
                tiles.append(jnp.where(high, mine, theirs) if north_side else jnp.where(high, theirs, mine))
            return tiles
        u_side, v_side = side(0), side(1)
        steps = []
        for t in u_side:
            t = jnp.where(t > 0.0, t, 1.0)
            have = 1
            while have < per_tile:
                t = jnp.where(slot_id >= per_tile - have, t, lane_roll(t, -SLOT * have))
                have *= 2
            steps.append((0.5 * last) / t)
        mu = []
        grads = []
        for pair in (u_side, v_side):
            e = [sub_roll(jnp.where(sub_first, pair[1 - h], pair[h]), -1) for h in range(2)]
            w = [sub_roll(jnp.where(sub_last, pair[1 - h], pair[h]), 1) for h in range(2)]
            for h in range(2):
                t = pair[h]
                n, s = lane_roll(t, -1), lane_roll(t, 1)
                above = jnp.where(slot_id == last, t, lane_roll(t, -SLOT))
                below = jnp.where(slot_id == 0, t, lane_roll(t, SLOT))
                grads.append((0.5 * (e[h] - w[h]), 0.5 * (n - s), (above - below) * steps[h]))
        for h in range(2):
            mu.append(viscosity(*grads[h], *grads[2 + h]))
        strips.append(mu)
    mu_packs = [jnp.where(high, strips[1][h], strips[0][h]) for h in range(2)]

    half_step = Field((0.5 * inverse_step).tiles[:2] + [None, None])
    velocity = []
    for c in range(2):
        for l in range(layers):
            velocity.append(assemble(c * per_tile + l))
    visc = []
    for l in range(layers):
        grads = []
        for c in range(2):
            f = velocity[c * layers + l]
            main = Field(f.tiles[:2] + [None, None])
            gx = 0.5 * (neighbour(main, EAST) - neighbour(main, WEST))
            gy = 0.5 * (neighbour(f, NORTH) - neighbour(f, SOUTH))
            gz = (velocity[c * layers + min(l + 1, last)] - velocity[c * layers + max(l - 1, 0)]) * half_step
            grads.append((gx, gy, gz))
        (ux, uy, uz), (vx, vy, vz) = grads
        tiles = [
            viscosity(ux.tiles[h], uy.tiles[h], uz.tiles[h], vx.tiles[h], vy.tiles[h], vz.tiles[h]) for h in range(2)
        ]
        visc.append(Field(tiles + strip(mu_packs, l)))

    def store(ref, index, f):
        for k, t in enumerate(f.tiles):
            if t is not None:
                ref[index + (k,)] = t

    def load(ref, index, count=4):
        return Field([ref[index + (k,)] if k < count else None for k in range(4)])

    for c in range(2):
        store(drv, (c,), friction * velocity[c * layers])
    store(wmx, (), wm)
    for p in range(probes):
        for h, t in enumerate(strip(both_packs[2], p)):
            probe_strip[p, pl.ds(h * rows, rows), :] = t

    mask_e = 0.5 * (mask * neighbour(mask, EAST))
    mask_n = 0.5 * (mask * neighbour(mask, NORTH))
    step2 = 0.5 * (inverse_step * inverse_step * mask)
    diag = MASS_TERM * mask + mask.map(lambda t: 1.0 - t)
    for l in range(layers):
        mu = visc[l]
        k_e = (mu + neighbour(mu, EAST)) * mask_e
        k_n = (mu + neighbour(mu, NORTH)) * mask_n
        for d, f in ((WEST, neighbour(k_e, WEST)), (EAST, k_e), (SOUTH, neighbour(k_n, SOUTH)), (NORTH, k_n)):
            store(coef, (d, l), f)
        if l < last:
            store(kzs, (l,), (mu + visc[l + 1]) * step2)

    for c in range(2):
        ratios, inverses = [], []
        for l in range(layers):
            k = [load(coef, (d, l)) for d in DIRS]
            pivot = ANISO_X[c] * (k[WEST] + k[EAST]) + ANISO_Y[c] * (k[SOUTH] + k[NORTH]) + diag
            if l == 0:
                pivot = pivot + friction
            if l > 0:
                below = load(kzs, (l - 1,))
                pivot = pivot + below
            if l < last:
                pivot = pivot + load(kzs, (l,))
            if l > 0:
                pivot = pivot - below * ratios[-1]
            inv = pivot.map(lambda t: 1.0 / t)
            inverses.append(inv)
            store(inverse, (c, l), inv)
            if l < last:
                ratios.append(load(kzs, (l,)) * inv)
                store(ratio, (c, l), ratios[-1])
        up = [inverses[0]]
        for l in range(1, layers):
            up.append(load(kzs, (l - 1,)) * up[-1] * inverses[l])
        from_bottom, from_top = up[last], inverses[last]
        for l in range(last, -1, -1):
            if l < last:
                from_bottom = up[l] + ratios[l] * from_bottom
                from_top = ratios[l] * from_top
            store(green, (0, c, l), from_bottom)
            store(green, (1, c, l), from_top)

    def prepare(p):
        src = 0 if p == 0 else last
        for c in range(2):
            scale = (ANISO_X[c], ANISO_X[c], ANISO_Y[c], ANISO_Y[c])
            for d in DIRS:
                y = []
                for l in range(layers):
                    w = scale[d] * (load(coef, (d, l)) * neighbour(load(green, (p, c, l)), d))
                    wsc[c, d, l] = w.tiles[0]
                    if p == 1:
                        w = Field(w.tiles[:3] + [None])
                    if l > 0:
                        w = w + load(kzs, (l - 1,)) * y[-1]
                    y.append(w * load(inverse, (c, l)))
                x = y[last]
                for l in range(last, -1, -1):
                    if l < last:
                        x = Field((y[l] + load(ratio, (c, l)) * x).tiles[:3] + [None])
                    store(hsc, (p, c, d, l), x)
                    hshift[c, 0, d, l] = sub_roll(jnp.where(sub_first, x.tiles[1], x.tiles[0]), -1)
                    hshift[c, 1, d, l] = lane_roll(jnp.where(lane_first, x.tiles[2], x.tiles[0]), -1)
            quad[p, c, 0] = green[p, c, src, 0]
            for d in DIRS:
                quad[p, c, 1 + d] = hsc[p, c, d, src, 0]
            at = 1 + len(DIRS)
            for d in DIRS:
                for e in range(d, 4):
                    total = None
                    for l in range(layers):
                        term = wsc[c, d, l] * hsc[p, c, e, l, 0]
                        total = term if total is None else total + term
                    quad[p, c, at] = total
                    at += 1
            for d in DIRS:
                total = [None] * 6
                for l in range(layers):
                    h = hsc[p, c, d, l, 0]
                    t_e = (ANISO_X[c] * coef[EAST, l, 0]) * h
                    t_n = (ANISO_Y[c] * coef[NORTH, l, 0]) * h
                    he = [hshift[c, 0, e, l] for e in DIRS]
                    hn = [hshift[c, 1, e, l] for e in DIRS]
                    terms = [
                        t_e * he[WEST] + t_n * hn[SOUTH], t_e * he[EAST], t_e * he[SOUTH],
                        t_e * he[NORTH] + t_n * hn[EAST], t_n * hn[WEST], t_n * hn[NORTH],
                    ]
                    total = [b if a is None else a + b for a, b in zip(total, terms)]
                for k in range(6):
                    quad[p, c, at] = total[k]
                    at += 1

    def where_row(r):
        return (0, r) if 0 <= r < rows else (1, r % rows)

    def main_strip(ref, index, r):
        h, at = where_row(r)
        return ref[index + (h, pl.ds(at, 1), slice(None))], ref[index + (2 + h, pl.ds(at, 1), slice(None))]

    def north_of(m, s):
        return lane_roll(jnp.where(lane_first, s, m), -1)

    def south_of(m, s):
        return lane_roll(jnp.where(lane_last, s, m), 1)

    def b_of(p, c, r, s=0):
        return bx[p, c, r + 2, s]

    def grams_of(p):
        for c in range(2):
            for i in range(rows):
                k = pl.ds((c * rows + i) * lanes, lanes)
                q = quad.at[p, c]

                def row_of(index):
                    return q[index, pl.ds(i, 1), :]

                b0 = b_of(p, c, i)
                n_w, n_0, n_e = (north_of(b_of(p, c, i + d), b_of(p, c, i + d, 1)) for d in (-1, 0, 1))
                s_0, s_e = (south_of(b_of(p, c, i + d), b_of(p, c, i + d, 1)) for d in (0, 1))
                n_2 = lane_roll(jnp.where(lane < 2, b_of(p, c, i, 1), b0), -2)
                around = [b_of(p, c, i - 1), b_of(p, c, i + 1), s_0, n_0]
                far = [b0, b_of(p, c, i + 2), s_e, n_e, n_w, n_2]
                left[0, :, k] = b0
                right[0, 0:probes, k] = row_of(0) * b0
                first = [row_of(1 + d) * around[d] for d in DIRS]
                right[0, probes:, k] = (first[0] + first[1]) + (first[2] + first[3])
                at = 1 + len(DIRS)
                cross = {}
                for d in DIRS:
                    for e in range(d, 4):
                        cross[d, e] = cross[e, d] = row_of(at)
                        at += 1
                for d in DIRS:
                    left[1 + d, :, k] = around[d]
                    terms = [cross[d, e] * around[e] for e in DIRS]
                    right[1 + d, 0:probes, k] = (terms[0] + terms[1]) + (terms[2] + terms[3])
                    terms = [row_of(at + j) * far[j] for j in range(6)]
                    at += 6
                    right[1 + d, probes:, k] = (terms[0] + terms[1]) + (terms[2] + terms[3]) + (terms[4] + terms[5])
        dots = [
            lax.dot_general(
                left[k], right[k], (((1,), (1,)), ((), ())), precision=HIGHEST, preferred_element_type=jnp.float32
            )
            for k in range(5)
        ]
        outer = (dots[1] + dots[2]) + (dots[3] + dots[4])
        pad = jnp.zeros((probes, lanes - FORMS * probes), jnp.float32)
        return jnp.concatenate([dots[0], outer, pad], axis=1)

    def start_sum(p, grams):
        base = (FORMS - 1) * probes
        mirrored = grams
        for r in range(probes):
            column = jnp.sum(
                jnp.where(lane == base + sub, jnp.broadcast_to(grams[r : r + 1, :], tile), 0.0), axis=1, keepdims=True
            )
            mirrored = jnp.where(lane == base + r, grams + column, mirrored)
        grams = mirrored
        width = FORMS * probes
        packed = grams
        for q in range(1, probes // PAIR):
            packed = jnp.where(lane < q * width, packed, lane_roll(sub_roll(grams, -PAIR * q), q * width))
        mine = pl.ds((ix * n_gy + iy) * PAIR, PAIR)
        landed[p, mine, :] = packed[0:PAIR, :]
        tile_src[p] = packed[0:PAIR, :]
        for peer in peers:
            pltpu.make_async_remote_copy(
                src_ref=tile_src.at[p], dst_ref=landed.at[p, mine], send_sem=ar_send.at[p], recv_sem=ar_recv.at[p],
                device_id=peer, device_id_type=MESH,
            ).start()

    def everyone(p):
        total_rows = pl.ds(0, PAIR * len(peers))
        return pltpu.make_async_remote_copy(
            src_ref=landed.at[p, total_rows], dst_ref=landed.at[p, total_rows], send_sem=ar_send.at[p],
            recv_sem=ar_recv.at[p], device_id=peers[0], device_id_type=MESH,
        )

    def mixing_of(p):
        everyone(p).wait_recv()
        parts = [landed[p, k * probes : (k + 1) * probes, :] for k in range(landed.shape[1] // probes)]
        while len(parts) > 1:
            parts = [parts[k] + parts[k + 1] if k + 1 < len(parts) else parts[k] for k in range(0, len(parts), 2)]
        packed = parts[0]
        shift = PAIR
        while shift < probes:
            packed = packed + sub_roll(packed, shift)
            shift *= 2
        grams = packed
        for q in range(1, probes // PAIR):
            grams = jnp.where(sub < PAIR * q, grams, lane_roll(packed, -q * FORMS * probes))
        diff = grams - lane_roll(grams, -probes)
        upper = jnp.where(lane < 2 * probes, diff, lane_roll(grams, 2 * probes))
        lower = jnp.where(lane < 2 * probes, lane_roll(diff, -probes), lane_roll(grams, probes))
        size = 2 * probes
        both = [upper, lower]
        scale = [jnp.sum(jnp.where(lane == sub + h * probes, both[h], 0.0), axis=1, keepdims=True) for h in range(2)]
        for k in range(size):
            h, r = k // probes, k % probes
            line = both[h][r : r + 1, :]
            pivot = line[:, k : k + 1]
            inv = jnp.where(pivot > 1e-6 * scale[h][r : r + 1, :], 1.0 / pivot, 0.0)
            line = line * inv
            for q in range(2):
                updated = both[q] - both[q][:, k : k + 1] * line
                both[q] = jnp.where(sub == r, line, updated) if q == h else updated
        pick = (lane == sub + size).astype(jnp.float32)
        return lax.dot_general(
            pick, jnp.concatenate(both, axis=0), (((1,), (1,)), ((), ())),
            precision=HIGHEST, preferred_element_type=jnp.float32,
        )

    def mix(mixing, stacked):
        return lax.dot_general(
            mixing, stacked, (((1,), (0,)), ((), ())), precision=HIGHEST, preferred_element_type=jnp.float32
        )

    prepare(0)
    for r in range(-2, rows + 2):
        h, at = where_row(r)
        main = probes_ref[:, at, :] if h == 0 else hrow[2 * per_tile : 2 * per_tile + probes, at, :]
        side = probe_strip[:, h * rows + at, :]
        for c in range(2):
            d_main, d_side = main_strip(drv, (c,), r)
            bx[0, c, r + 2, 0] = main * d_main
            bx[0, c, r + 2, 1] = side * d_side

    span = rows + 3

    def place(c, r, s):
        return pl.ds(((c * span + r + 1) * 2 + s) * lanes, lanes)

    for c in range(2):
        for r in range(-1, rows + 2):
            g = main_strip(green, (0, c, last), r)
            w = main_strip(wmx, (), r)
            m, s = b_of(0, c, r), b_of(0, c, r, 1)
            basis[0:probes, place(c, r, 0)] = (g[0] * w[0]) * m
            basis[0:probes, place(c, r, 1)] = (g[1] * w[1]) * s
            if r > rows:
                continue
            sides = [
                (b_of(0, c, r - 1), b_of(0, c, r - 1, 1)), (b_of(0, c, r + 1), b_of(0, c, r + 1, 1)),
                (south_of(m, s), south_of(s, m)), (north_of(m, s), north_of(s, m)),
            ]
            hs = [main_strip(hsc, (0, c, d, last), r) for d in DIRS]
            for k in range(2):
                x = (hs[0][k] * sides[0][k] + hs[1][k] * sides[1][k]) + (hs[2][k] * sides[2][k] + hs[3][k] * sides[3][k])
                if r == 1:
                    edge_src[c, k] = x
                basis[probes:, place(c, r, k)] = w[k] * x
    pl.when(edge_copy[2])(edge_copy[0].start)
    start_sum(0, grams_of(0))
    prepare(1)
    pl.when(edge_copy[3])(edge_copy[0].wait_recv)
    for c in range(2):
        w = main_strip(wmx, (), rows + 1)
        for k in range(2):
            basis[probes:, place(c, rows + 1, k)] = w[k] * edge_dst[c, k]
    mixing = mixing_of(0)
    mixed = mix(mixing, basis[...])
    for c in range(2):
        for r in range(-1, rows + 2):
            for k in range(2):
                start = ((c * span + r + 1) * 2 + k) * lanes
                bx[1, c, r + 2, k] = mixed[:, start : start + lanes]
    start_sum(1, grams_of(1))
    for i in range(rows):
        total = [None, None]
        for c in range(2):
            drive = drv[c, 0, pl.ds(i, 1), :]
            m, s = b_of(1, c, i), b_of(1, c, i, 1)
            around = [b_of(1, c, i - 1), b_of(1, c, i + 1), south_of(m, s), north_of(m, s)]
            terms = [hsc[1, c, d, 0, 0, pl.ds(i, 1), :] * around[d] for d in DIRS]
            parts = [
                (drive * green[1, c, 0, 0, pl.ds(i, 1), :]) * m,
                drive * ((terms[0] + terms[1]) + (terms[2] + terms[3])),
            ]
            total = [b if a is None else a + b for a, b in zip(total, parts)]
        for k in range(2):
            results[k * probes : (k + 1) * probes, pl.ds(i * lanes, lanes)] = total[k]
    mixed = mix(mixing_of(1), results[...])
    for i in range(rows):
        out_ref[:, i, :] = mixed[:, i * lanes : (i + 1) * lanes]
    for copy, _, has_dst, _ in exchange + [edge_copy]:
        pl.when(has_dst)(copy.wait_send)
    for p in range(2):
        everyone(p).wait_send()


def body(sizes, velocity, thickness, log_friction, obs_weight, ice_mask, grounded, probes):
    layers, rows, lanes = velocity.shape[1:]
    count = probes.shape[0]
    n_gx, n_gy = sizes
    fields = 2 * (layers + 1) + count + 2 + 3
    forms = 1 + 4 + 10 + 24

    def vmem(*shape):
        return pltpu.VMEM(shape, jnp.float32)

    sem = pltpu.SemaphoreType.DMA
    scratch = [
        vmem(fields, rows, lanes), vmem(fields, rows, lanes), vmem(3, 2 * rows, lanes), vmem(3, 2 * rows, lanes),
        vmem(2, 2, count, lanes), vmem(2, 2, count, lanes),
        vmem(4, layers, 4, rows, lanes), vmem(layers - 1, 4, rows, lanes), vmem(2, layers - 1, 4, rows, lanes),
        vmem(2, layers, 4, rows, lanes), vmem(2, 2, layers, 4, rows, lanes), vmem(2, 4, layers, rows, lanes),
        vmem(2, 2, 4, layers, 4, rows, lanes), vmem(2, 2, 4, layers, rows, lanes), vmem(2, 2, forms, rows, lanes),
        vmem(2, 4, rows, lanes), vmem(4, rows, lanes), vmem(count, 2 * rows, lanes),
        vmem(2, 2, rows + 4, 2, count, lanes), vmem(5, count, 2 * rows * lanes), vmem(5, 2 * count, 2 * rows * lanes),
        vmem(2 * count, 4 * (rows + 3) * lanes), vmem(2 * count, rows * lanes),
        vmem(2, PAIR, lanes), vmem(2, PAIR * n_gx * n_gy, lanes),
        sem((9,)), sem((9,)), sem((2,)), sem((2,)),
    ]
    return pl.pallas_call(
        functools.partial(kernel, sizes),
        out_shape=jax.ShapeDtypeStruct(probes.shape, jnp.float32),
        in_specs=[pl.BlockSpec(memory_space=pltpu.VMEM)] * 7,
        out_specs=pl.BlockSpec(memory_space=pltpu.VMEM),
        scratch_shapes=scratch,
        compiler_params=pltpu.CompilerParams(collective_id=0, has_side_effects=True),
        name="hessian_probe",
    )(velocity, thickness, log_friction, obs_weight, ice_mask, grounded, probes)


def solution(mesh):
    sizes = (mesh.shape["gx"], mesh.shape["gy"])
    in_specs = (
        P(None, None, "gx", "gy"),
        P("gx", "gy"),
        P("gx", "gy"),
        P("gx", "gy"),
        P("gx", "gy"),
        P("gx", "gy"),
        P(None, "gx", "gy"),
    )
    out_specs = P(None, "gx", "gy")
    return jax.shard_map(
        functools.partial(body, sizes), mesh=mesh, in_specs=in_specs, out_specs=out_specs, check_vma=False
    )
```

```python
import functools

import jax
import jax.numpy as jnp
from jax import lax
from jax.experimental import pallas as pl
from jax.experimental.pallas import tpu as pltpu
from jax.sharding import PartitionSpec as P

MASS_TERM = 0.1
STRAIN_OFFSET = 0.01
ANISO_X = (4.0, 1.0)
ANISO_Y = (1.0, 4.0)
HIGHEST = lax.Precision.HIGHEST
MESH = pl.DeviceIdType.MESH
PAIR = 2
REACH = 5
SLOT = 2 * REACH
WEST, EAST, SOUTH, NORTH = range(4)
DIRS = range(4)
FORMS = 4


def rounds_of(count):
    rounds = 0
    while 2 ** (rounds + 1) < count - 1:
        rounds += 1
    return rounds


class Field:
    def __init__(self, tiles):
        self.tiles = tiles

    def _with(self, other, op):
        if isinstance(other, Field):
            return Field([None if a is None or b is None else op(a, b) for a, b in zip(self.tiles, other.tiles)])
        return Field([None if a is None else op(a, other) for a in self.tiles])

    def __add__(self, other):
        return self._with(other, lambda a, b: a + b)

    def __sub__(self, other):
        return self._with(other, lambda a, b: a - b)

    def __mul__(self, other):
        return self._with(other, lambda a, b: a * b)

    __radd__ = __add__
    __rmul__ = __mul__

    def map(self, op):
        return Field([None if a is None else op(a) for a in self.tiles])


def kernel(
    sizes,
    vel_hbm, thick_hbm, logf_hbm, obs_hbm, ice_hbm, ground_hbm, probes_hbm,
    out_ref,
    vel_ref, thick_ref, logf_ref, obs_ref, ice_ref, ground_ref, probes_ref,
    row, hrow, tn, ts, edge_src, edge_dst,
    coef, kzs, ratio, inverse, green, wsc, hsc, hshift, quad, drv, wmx, probe_strip,
    bx, left, right, basis, results, tile_src, landed,
    send_sem, recv_sem, ar_send, ar_recv, in_sem, greet_sem,
):
    n_gx, n_gy = sizes
    loads = [
        pltpu.make_async_copy(src, dst, in_sem.at[k])
        for k, (src, dst) in enumerate((
            (vel_hbm, vel_ref), (probes_hbm, probes_ref), (thick_hbm, thick_ref), (logf_hbm, logf_ref),
            (obs_hbm, obs_ref), (ice_hbm, ice_ref), (ground_hbm, ground_ref),
        ))
    ]
    for copy in loads:
        copy.start()
    layers = vel_ref.shape[1]
    rows = vel_ref.shape[2]
    lanes = vel_ref.shape[3]
    probes = probes_ref.shape[0]
    last = layers - 1
    half = rows // 2
    per_tile = layers + 1
    n_fields = 2 * per_tile + probes + 2
    ix = lax.axis_index("gx")
    iy = lax.axis_index("gy")
    tile = (rows, lanes)
    lane = lax.broadcasted_iota(jnp.int32, tile, 1)
    sub = lax.broadcasted_iota(jnp.int32, tile, 0)
    lane_first = lane == 0
    lane_last = lane == lanes - 1
    sub_first = sub == 0
    sub_last = sub == rows - 1
    slot_id = lane // SLOT
    high = lane - slot_id * SLOT < REACH

    barrier = pltpu.get_barrier_semaphore()
    peers = [
        {"gx": lax.rem(ix + step // n_gy, n_gx), "gy": lax.rem(iy + step % n_gy, n_gy)} for step in range(1, n_gx * n_gy)
    ]
    def lane_roll(t, shift):
        shift = shift % lanes
        return t if shift == 0 else pltpu.roll(t, shift, 1)

    def sub_roll(t, shift):
        return pltpu.roll(t, shift % rows, 0)

    def inside(dx, dy):
        tests = []
        if dx:
            tests.append(ix >= -dx if dx < 0 else ix < n_gx - dx)
        if dy:
            tests.append(iy >= -dy if dy < 0 else iy < n_gy - dy)
        return functools.reduce(jnp.logical_and, tests)

    def transfer(k, dx, dy, src, dst):
        target = {}
        if dx:
            target["gx"] = ix + dx
        if dy:
            target["gy"] = iy + dy
        copy = pltpu.make_async_remote_copy(
            src_ref=src, dst_ref=dst, send_sem=send_sem.at[k], recv_sem=recv_sem.at[k],
            device_id=target, device_id_type=MESH,
        )
        return copy, dst, inside(dx, dy), inside(-dx, -dy)

    for dy in (0, -1, 1, -2, 2):
        for step in range(n_gx):
            if step == 0 and dy == 0:
                continue
            target = {"gx": lax.rem(ix + step, n_gx), "gy": iy + dy}
            if dy == 0:
                pl.semaphore_signal(barrier, inc=1, device_id=target, device_id_type=MESH)
            else:
                @pl.when(inside(0, dy))
                def _(target=target):
                    pl.semaphore_signal(barrier, inc=1, device_id=target, device_id_type=MESH)
    low, top = pl.ds(0, half), pl.ds(half, half)
    corner_low, corner_top = pl.ds(rows, half), pl.ds(rows + half, half)
    own_pack = pl.ds(n_fields, 3)
    whole = pl.ds(0, rows)
    everything = pl.ds(0, n_fields + 3)
    packs = pl.ds(0, 3)
    exchange = [
        transfer(0, -1, 0, row.at[everything, low], hrow.at[everything, low]),
        transfer(1, 1, 0, row.at[everything, top], hrow.at[everything, top]),
        transfer(2, 0, -1, row.at[own_pack, whole], tn.at[packs, whole]),
        transfer(3, 0, 1, row.at[own_pack, whole], ts.at[packs, whole]),
        transfer(4, -1, -1, row.at[own_pack, low], tn.at[packs, corner_low]),
        transfer(5, 1, -1, row.at[own_pack, top], tn.at[packs, corner_top]),
        transfer(6, -1, 1, row.at[own_pack, low], ts.at[packs, corner_low]),
        transfer(7, 1, 1, row.at[own_pack, top], ts.at[packs, corner_top]),
    ]
    edge_copy = transfer(8, -1, 0, edge_src, edge_dst)

    for copy in loads:
        copy.wait()
    mask_own = ice_ref[...].astype(jnp.float32)
    friction_own = mask_own * ground_ref[...].astype(jnp.float32) * jnp.exp(logf_ref[...])
    wm_own = obs_ref[...] * mask_own
    own = [vel_ref[0, l] for l in range(layers)] + [thick_ref[...]]
    own += [vel_ref[1, l] for l in range(layers)] + [mask_own]
    own += [probes_ref[p] for p in range(probes)] + [friction_own, wm_own]
    for f, t in enumerate(own):
        row[f] = t
    for k in range(3):
        packed = None
        for s, t in enumerate(own[k * per_tile : (k + 1) * per_tile]):
            moved = lane_roll(t, s * SLOT + REACH)
            packed = moved if packed is None else jnp.where(slot_id == s, moved, packed)
        row[n_fields + k] = packed

    for _, dst, _, has_src in exchange + [edge_copy]:
        @pl.when(jnp.logical_not(has_src))
        def _(dst=dst):
            dst[...] = jnp.zeros(dst.shape, jnp.float32)
    within = sum(inside(0, dy).astype(jnp.int32) for dy in (-1, 1, -2, 2)) + 1
    pl.semaphore_wait(barrier, n_gx * within - 1)
    for copy, _, has_dst, _ in exchange:
        pl.when(has_dst)(copy.start)

    def greet(k):
        for dy in (-(2 ** (k + 1)), 2 ** (k + 1)):
            @pl.when(inside(0, dy))
            def _(dy=dy):
                pl.semaphore_signal(greet_sem.at[k], inc=1, device_id={"gy": iy + dy}, device_id_type=MESH)

    def meet(k):
        if k < rounds:
            reach = 2 ** (k + 1)
            pl.semaphore_wait(
                greet_sem.at[k], inside(0, -reach).astype(jnp.int32) + inside(0, reach).astype(jnp.int32)
            )
        if k + 1 < rounds:
            greet(k + 1)

    rounds = rounds_of(n_gy)
    if rounds:
        greet(0)
    meet(0)
    for copy, _, _, has_src in exchange:
        pl.when(has_src)(copy.wait_recv)

    def shifted(f, axis, forward):
        if axis == 0:
            at, move, pairs = (sub_first, -1, ((0, 1), (1, 0), (2, 3), (3, 2))) if forward else (sub_last, 1, ((0, 1), (1, 0), (2, 3), (3, 2)))
            roll = sub_roll
        else:
            at, move, pairs = (lane_first, -1, ((0, 2), (1, 3), (2, 0), (3, 1))) if forward else (lane_last, 1, ((0, 2), (1, 3), (2, 0), (3, 1)))
            roll = lane_roll
        tiles = [None] * 4
        for a, b in pairs:
            if f.tiles[a] is not None and f.tiles[b] is not None:
                tiles[a] = roll(jnp.where(at, f.tiles[b], f.tiles[a]), move)
        return Field(tiles)

    def neighbour(f, d):
        return shifted(f, 0 if d in (WEST, EAST) else 1, d in (EAST, NORTH))

    both_packs = [
        [jnp.where(high, ts[k, pl.ds(h * rows, rows), :], tn[k, pl.ds(h * rows, rows), :]) for h in range(2)]
        for k in range(3)
    ]

    def strip(packs_of, s):
        return [lane_roll(t, -(s * SLOT + REACH)) for t in packs_of]

    def assemble(f):
        return Field([own[f], hrow[f]] + strip(both_packs[f // per_tile], f % per_tile))

    thick = assemble(layers).map(lambda t: jnp.where(t > 0.0, t, 1.0))
    inverse_step = thick.map(lambda t: last / t)
    mask = assemble(per_tile + layers)
    friction = assemble(2 * per_tile + probes)
    wm = assemble(2 * per_tile + probes + 1)

    def viscosity(ux, uy, uz, vx, vy, vz):
        shear = uy + vx
        strain = ux * ux + vy * vy + ux * vy + 0.25 * (shear * shear) + 0.25 * (uz * uz + vz * vz) + STRAIN_OFFSET
        root = jnp.exp(jnp.log(strain) * (-1.0 / 3.0))
        root = root + root * (1.0 - strain * root * root * root) * (1.0 / 3.0)
        return 0.5 * root

    strips = []
    for north_side in (True, False):
        def side(k):
            tiles = []
            for h in range(2):
                mine = row[n_fields + k] if h == 0 else hrow[n_fields + k]
                theirs = (tn if north_side else ts)[k, pl.ds(h * rows, rows), :]
                tiles.append(jnp.where(high, mine, theirs) if north_side else jnp.where(high, theirs, mine))
            return tiles
        u_side, v_side = side(0), side(1)
        steps = []
        for t in u_side:
            t = jnp.where(t > 0.0, t, 1.0)
            have = 1
            while have < per_tile:
                t = jnp.where(slot_id >= per_tile - have, t, lane_roll(t, -SLOT * have))
                have *= 2
            steps.append((0.5 * last) / t)
        mu = []
        grads = []
        for pair in (u_side, v_side):
            e = [sub_roll(jnp.where(sub_first, pair[1 - h], pair[h]), -1) for h in range(2)]
            w = [sub_roll(jnp.where(sub_last, pair[1 - h], pair[h]), 1) for h in range(2)]
            for h in range(2):
                t = pair[h]
                n, s = lane_roll(t, -1), lane_roll(t, 1)
                above = jnp.where(slot_id == last, t, lane_roll(t, -SLOT))
                below = jnp.where(slot_id == 0, t, lane_roll(t, SLOT))
                grads.append((0.5 * (e[h] - w[h]), 0.5 * (n - s), (above - below) * steps[h]))
        for h in range(2):
            mu.append(viscosity(*grads[h], *grads[2 + h]))
        strips.append(mu)
    mu_packs = [jnp.where(high, strips[1][h], strips[0][h]) for h in range(2)]

    half_step = Field((0.5 * inverse_step).tiles[:2] + [None, None])
    velocity = []
    for c in range(2):
        for l in range(layers):
            velocity.append(assemble(c * per_tile + l))
    visc = []
    for l in range(layers):
        grads = []
        for c in range(2):
            f = velocity[c * layers + l]
            main = Field(f.tiles[:2] + [None, None])
            gx = 0.5 * (neighbour(main, EAST) - neighbour(main, WEST))
            gy = 0.5 * (neighbour(f, NORTH) - neighbour(f, SOUTH))
            gz = (velocity[c * layers + min(l + 1, last)] - velocity[c * layers + max(l - 1, 0)]) * half_step
            grads.append((gx, gy, gz))
        (ux, uy, uz), (vx, vy, vz) = grads
        tiles = [
            viscosity(ux.tiles[h], uy.tiles[h], uz.tiles[h], vx.tiles[h], vy.tiles[h], vz.tiles[h]) for h in range(2)
        ]
        visc.append(Field(tiles + strip(mu_packs, l)))

    def store(ref, index, f):
        for k, t in enumerate(f.tiles):
            if t is not None:
                ref[index + (k,)] = t

    def load(ref, index, count=4):
        return Field([ref[index + (k,)] if k < count else None for k in range(4)])

    def scale_of(c, d):
        return ANISO_X[c] if d in (WEST, EAST) else ANISO_Y[c]

    for c in range(2):
        store(drv, (c,), friction * velocity[c * layers])
    store(wmx, (), wm)
    for p in range(probes):
        for h, t in enumerate(strip(both_packs[2], p)):
            probe_strip[p, pl.ds(h * rows, rows), :] = t

    mask_e = 0.5 * (mask * neighbour(mask, EAST))
    mask_n = 0.5 * (mask * neighbour(mask, NORTH))
    step2 = 0.5 * (inverse_step * inverse_step * mask)
    diag = MASS_TERM * mask + mask.map(lambda t: 1.0 - t)
    for l in range(layers):
        mu = visc[l]
        k_e = (mu + neighbour(mu, EAST)) * mask_e
        k_n = (mu + neighbour(mu, NORTH)) * mask_n
        for d, f in ((WEST, neighbour(k_e, WEST)), (EAST, k_e), (SOUTH, neighbour(k_n, SOUTH)), (NORTH, k_n)):
            for c in range(2):
                store(coef, (c, d, l), f if scale_of(c, d) == 1.0 else scale_of(c, d) * f)
        if l < last:
            store(kzs, (l,), (mu + visc[l + 1]) * step2)

    for c in range(2):
        ratios, inverses = [], []
        for l in range(layers):
            k = [load(coef, (c, d, l)) for d in DIRS]
            pivot = (k[WEST] + k[EAST]) + (k[SOUTH] + k[NORTH]) + diag
            if l == 0:
                pivot = pivot + friction
            if l > 0:
                below = load(kzs, (l - 1,))
                pivot = pivot + below
            if l < last:
                pivot = pivot + load(kzs, (l,))
            if l > 0:
                pivot = pivot - below * ratios[-1]
            inv = pivot.map(lambda t: 1.0 / t)
            inverses.append(inv)
            store(inverse, (c, l), inv)
            if l < last:
                ratios.append(load(kzs, (l,)) * inv)
                store(ratio, (c, l), ratios[-1])
        up = [inverses[0]]
        for l in range(1, layers):
            up.append(load(kzs, (l - 1,)) * up[-1] * inverses[l])
        from_bottom, from_top = up[last], inverses[last]
        for l in range(last, -1, -1):
            if l < last:
                from_bottom = up[l] + ratios[l] * from_bottom
                from_top = ratios[l] * from_top
            store(green, (0, c, l), from_bottom)
            store(green, (1, c, l), from_top)

    def prepare(p):
        src = 0 if p == 0 else last
        for c in range(2):
            for d in DIRS:
                y = []
                for l in range(layers):
                    w = load(coef, (c, d, l)) * neighbour(load(green, (p, c, l)), d)
                    wsc[c, d, l] = w.tiles[0]
                    if p == 1:
                        w = Field(w.tiles[:3] + [None])
                    if l > 0:
                        w = w + load(kzs, (l - 1,)) * y[-1]
                    y.append(w * load(inverse, (c, l)))
                x = y[last]
                for l in range(last, -1, -1):
                    if l < last:
                        x = Field((y[l] + load(ratio, (c, l)) * x).tiles[:3] + [None])
                    store(hsc, (p, c, d, l), x if p == 0 and l == last else Field(x.tiles[:1] + [None] * 3))
                    hshift[c, 0, d, l] = sub_roll(jnp.where(sub_first, x.tiles[1], x.tiles[0]), -1)
                    hshift[c, 1, d, l] = lane_roll(jnp.where(lane_first, x.tiles[2], x.tiles[0]), -1)
            quad[p, c, 0] = green[p, c, src, 0]
            for d in DIRS:
                quad[p, c, 1 + d] = hsc[p, c, d, src, 0]
            at = 1 + len(DIRS)
            for d in DIRS:
                for e in range(d, 4):
                    total = None
                    for l in range(layers):
                        term = wsc[c, d, l] * hsc[p, c, e, l, 0]
                        total = term if total is None else total + term
                    quad[p, c, at] = total
                    at += 1
            for d in DIRS:
                total = [None] * 6
                for l in range(layers):
                    h = hsc[p, c, d, l, 0]
                    t_e = coef[c, EAST, l, 0] * h
                    t_n = coef[c, NORTH, l, 0] * h
                    he = [hshift[c, 0, e, l] for e in DIRS]
                    hn = [hshift[c, 1, e, l] for e in DIRS]
                    terms = [
                        t_e * he[WEST] + t_n * hn[SOUTH], t_e * he[EAST], t_e * he[SOUTH],
                        t_e * he[NORTH] + t_n * hn[EAST], t_n * hn[WEST], t_n * hn[NORTH],
                    ]
                    total = [b if a is None else a + b for a, b in zip(total, terms)]
                for k in range(6):
                    quad[p, c, at] = total[k]
                    at += 1

    def where_row(r):
        return (0, r) if 0 <= r < rows else (1, r % rows)

    def main_strip(ref, index, r):
        h, at = where_row(r)
        return ref[index + (h, pl.ds(at, 1), slice(None))], ref[index + (2 + h, pl.ds(at, 1), slice(None))]

    def north_of(m, s):
        return lane_roll(jnp.where(lane_first, s, m), -1)

    def south_of(m, s):
        return lane_roll(jnp.where(lane_last, s, m), 1)

    def b_of(p, c, r, s=0):
        return bx[p, c, r + 2, s]

    def remainder(t):
        return t - t.astype(jnp.bfloat16).astype(jnp.float32)

    def halves(t):
        return jnp.concatenate([t, remainder(t)], axis=0).astype(jnp.bfloat16)

    def at_k(block, c, i):
        return pl.ds(((block * 2 + c) * rows + i) * lanes, lanes)

    def put(block, c, i, one, two):
        t = jnp.concatenate([one, two], axis=0)
        right[0 : 2 * probes, at_k(block, c, i)] = t.astype(jnp.bfloat16)
        right[2 * probes :, at_k(block, c, i)] = remainder(t).astype(jnp.bfloat16)

    def grams_of(p):
        for c in range(2):
            for i in range(rows):
                q = quad.at[p, c]

                def row_of(index):
                    return q[index, pl.ds(i, 1), :]

                b0 = b_of(p, c, i)
                n_w, n_0, n_e = (north_of(b_of(p, c, i + d), b_of(p, c, i + d, 1)) for d in (-1, 0, 1))
                s_0, s_e = (south_of(b_of(p, c, i + d), b_of(p, c, i + d, 1)) for d in (0, 1))
                n_2 = lane_roll(jnp.where(lane < 2, b_of(p, c, i, 1), b0), -2)
                around = [b_of(p, c, i - 1), b_of(p, c, i + 1), s_0, n_0]
                far = [b0, b_of(p, c, i + 2), s_e, n_e, n_w, n_2]
                left[:, at_k(0, c, i)] = halves(b0)
                first = [row_of(1 + d) * around[d] for d in DIRS]
                put(0, c, i, row_of(0) * b0, (first[0] + first[1]) + (first[2] + first[3]))
                at = 1 + len(DIRS)
                cross = {}
                for d in DIRS:
                    for e in range(d, 4):
                        cross[d, e] = cross[e, d] = row_of(at)
                        at += 1
                for d in DIRS:
                    left[:, at_k(1 + d, c, i)] = halves(around[d])
                    terms = [cross[d, e] * around[e] for e in DIRS]
                    near = (terms[0] + terms[1]) + (terms[2] + terms[3])
                    terms = [row_of(at + j) * far[j] for j in range(6)]
                    at += 6
                    put(1 + d, c, i, near, (terms[0] + terms[1]) + (terms[2] + terms[3]) + (terms[4] + terms[5]))
        cut = 2 * rows * lanes

        def contract(at, size):
            both = lax.dot_general(
                left[:, pl.ds(at, size)], right[:, pl.ds(at, size)], (((1,), (1,)), ((), ())),
                preferred_element_type=jnp.float32,
            )
            both = both[0:probes, :] + both[probes:, :]
            return both[:, 0 : 2 * probes] + both[:, 2 * probes :]

        pad = jnp.zeros((probes, lanes - FORMS * probes), jnp.float32)
        return jnp.concatenate([contract(0, cut), contract(cut, 4 * cut), pad], axis=1)

    def start_sum(p, grams):
        base = (FORMS - 1) * probes
        mirrored = grams
        for r in range(probes):
            column = jnp.sum(
                jnp.where(lane == base + sub, jnp.broadcast_to(grams[r : r + 1, :], tile), 0.0), axis=1, keepdims=True
            )
            mirrored = jnp.where(lane == base + r, grams + column, mirrored)
        grams = mirrored
        width = FORMS * probes
        packed = grams
        for q in range(1, probes // PAIR):
            packed = jnp.where(lane < q * width, packed, lane_roll(sub_roll(grams, -PAIR * q), q * width))
        mine = pl.ds((ix * n_gy + iy) * PAIR, PAIR)
        landed[p, mine, :] = packed[0:PAIR, :]
        tile_src[p] = packed[0:PAIR, :]
        for peer in peers:
            pltpu.make_async_remote_copy(
                src_ref=tile_src.at[p], dst_ref=landed.at[p, mine], send_sem=ar_send.at[p], recv_sem=ar_recv.at[p],
                device_id=peer, device_id_type=MESH,
            ).start()

    def everyone(p):
        total_rows = pl.ds(0, PAIR * len(peers))
        return pltpu.make_async_remote_copy(
            src_ref=landed.at[p, total_rows], dst_ref=landed.at[p, total_rows], send_sem=ar_send.at[p],
            recv_sem=ar_recv.at[p], device_id=peers[0], device_id_type=MESH,
        )

    def mixing_of(p):
        everyone(p).wait_recv()
        parts = [landed[p, k * probes : (k + 1) * probes, :] for k in range(landed.shape[1] // probes)]
        while len(parts) > 1:
            parts = [parts[k] + parts[k + 1] if k + 1 < len(parts) else parts[k] for k in range(0, len(parts), 2)]
        packed = parts[0]
        shift = PAIR
        while shift < probes:
            packed = packed + sub_roll(packed, shift)
            shift *= 2
        grams = packed
        for q in range(1, probes // PAIR):
            grams = jnp.where(sub < PAIR * q, grams, lane_roll(packed, -q * FORMS * probes))
        diff = grams - lane_roll(grams, -probes)
        upper = jnp.where(lane < 2 * probes, diff, lane_roll(grams, 2 * probes))
        lower = jnp.where(lane < 2 * probes, lane_roll(diff, -probes), lane_roll(grams, probes))
        size = 2 * probes
        both = [upper, lower]
        scale = [jnp.sum(jnp.where(lane == sub + h * probes, both[h], 0.0), axis=1, keepdims=True) for h in range(2)]
        for k in range(size):
            h, r = k // probes, k % probes
            line = both[h][r : r + 1, :]
            pivot = line[:, k : k + 1]
            inv = jnp.where(pivot > 1e-6 * scale[h][r : r + 1, :], 1.0 / pivot, 0.0)
            line = line * inv
            for q in range(2):
                updated = both[q] - both[q][:, k : k + 1] * line
                both[q] = jnp.where(sub == r, line, updated) if q == h else updated
        pick = (lane == sub + size).astype(jnp.float32)
        return lax.dot_general(
            pick, jnp.concatenate(both, axis=0), (((1,), (1,)), ((), ())),
            precision=HIGHEST, preferred_element_type=jnp.float32,
        )

    def mix(mixing, stacked):
        return lax.dot_general(
            mixing, stacked, (((1,), (0,)), ((), ())), precision=HIGHEST, preferred_element_type=jnp.float32
        )

    prepare(0)
    for r in range(-2, rows + 2):
        h, at = where_row(r)
        main = probes_ref[:, at, :] if h == 0 else hrow[2 * per_tile : 2 * per_tile + probes, at, :]
        side = probe_strip[:, h * rows + at, :]
        for c in range(2):
            d_main, d_side = main_strip(drv, (c,), r)
            bx[0, c, r + 2, 0] = main * d_main
            bx[0, c, r + 2, 1] = side * d_side

    span = rows + 3

    def place(c, r, s):
        return pl.ds(((c * span + r + 1) * 2 + s) * lanes, lanes)

    def fill(c, r, s, one, two):
        t = jnp.concatenate([one, two], axis=0)
        basis[0 : 2 * probes, place(c, r, s)] = t.astype(jnp.bfloat16)
        basis[2 * probes :, place(c, r, s)] = remainder(t).astype(jnp.bfloat16)

    edge_plain = [None, None]
    for c in range(2):
        for r in range(-1, rows + 2):
            g = main_strip(green, (0, c, last), r)
            w = main_strip(wmx, (), r)
            m, s = b_of(0, c, r), b_of(0, c, r, 1)
            plain = [(g[0] * w[0]) * m, (g[1] * w[1]) * s]
            if r > rows:
                edge_plain[c] = plain
                continue
            sides = [
                (b_of(0, c, r - 1), b_of(0, c, r - 1, 1)), (b_of(0, c, r + 1), b_of(0, c, r + 1, 1)),
                (south_of(m, s), south_of(s, m)), (north_of(m, s), north_of(s, m)),
            ]
            hs = [main_strip(hsc, (0, c, d, last), r) for d in DIRS]
            for k in range(2):
                x = (hs[0][k] * sides[0][k] + hs[1][k] * sides[1][k]) + (hs[2][k] * sides[2][k] + hs[3][k] * sides[3][k])
                if r == 1:
                    edge_src[c, k] = x
                fill(c, r, k, plain[k], w[k] * x)
    pl.when(edge_copy[2])(edge_copy[0].start)
    grams = grams_of(0)
    for k in range(1, rounds):
        meet(k)
    start_sum(0, grams)
    prepare(1)
    pl.when(edge_copy[3])(edge_copy[0].wait_recv)
    for c in range(2):
        w = main_strip(wmx, (), rows + 1)
        for k in range(2):
            fill(c, rows + 1, k, edge_plain[c][k], w[k] * edge_dst[c, k])
    mixing = mixing_of(0)
    mixing = jnp.concatenate([mixing, mixing], axis=1)
    mixed = lax.dot_general(
        jnp.concatenate([mixing, remainder(mixing)], axis=0).astype(jnp.bfloat16), basis[...],
        (((1,), (0,)), ((), ())), preferred_element_type=jnp.float32,
    )
    mixed = mixed[0:probes, :] + mixed[probes:, :]
    for c in range(2):
        for r in range(-1, rows + 2):
            for k in range(2):
                start = ((c * span + r + 1) * 2 + k) * lanes
                bx[1, c, r + 2, k] = mixed[:, start : start + lanes]
    start_sum(1, grams_of(1))
    for i in range(rows):
        total = [None, None]
        for c in range(2):
            drive = drv[c, 0, pl.ds(i, 1), :]
            m, s = b_of(1, c, i), b_of(1, c, i, 1)
            around = [b_of(1, c, i - 1), b_of(1, c, i + 1), south_of(m, s), north_of(m, s)]
            terms = [hsc[1, c, d, 0, 0, pl.ds(i, 1), :] * around[d] for d in DIRS]
            parts = [
                (drive * green[1, c, 0, 0, pl.ds(i, 1), :]) * m,
                drive * ((terms[0] + terms[1]) + (terms[2] + terms[3])),
            ]
            total = [b if a is None else a + b for a, b in zip(total, parts)]
        for k in range(2):
            results[k * probes : (k + 1) * probes, pl.ds(i * lanes, lanes)] = total[k]
    mixed = mix(mixing_of(1), results[...])
    for i in range(rows):
        out_ref[:, i, :] = mixed[:, i * lanes : (i + 1) * lanes]
    for copy, _, has_dst, _ in exchange + [edge_copy]:
        pl.when(has_dst)(copy.wait_send)
    for p in range(2):
        everyone(p).wait_send()


def body(sizes, velocity, thickness, log_friction, obs_weight, ice_mask, grounded, probes):
    layers, rows, lanes = velocity.shape[1:]
    count = probes.shape[0]
    n_gx, n_gy = sizes
    fields = 2 * (layers + 1) + count + 2 + 3
    forms = 1 + 4 + 10 + 24

    def vmem(*shape):
        return pltpu.VMEM(shape, jnp.float32)

    sem = pltpu.SemaphoreType.DMA
    scratch = [
        vmem(*velocity.shape), vmem(rows, lanes), vmem(rows, lanes), vmem(rows, lanes),
        pltpu.VMEM((rows, lanes), jnp.int32), pltpu.VMEM((rows, lanes), jnp.int32), vmem(*probes.shape),
        vmem(fields, rows, lanes), vmem(fields, rows, lanes), vmem(3, 2 * rows, lanes), vmem(3, 2 * rows, lanes),
        vmem(2, 2, count, lanes), vmem(2, 2, count, lanes),
        vmem(2, 4, layers, 4, rows, lanes), vmem(layers - 1, 4, rows, lanes), vmem(2, layers - 1, 4, rows, lanes),
        vmem(2, layers, 4, rows, lanes), vmem(2, 2, layers, 4, rows, lanes), vmem(2, 4, layers, rows, lanes),
        vmem(2, 2, 4, layers, 4, rows, lanes), vmem(2, 2, 4, layers, rows, lanes), vmem(2, 2, forms, rows, lanes),
        vmem(2, 4, rows, lanes), vmem(4, rows, lanes), vmem(count, 2 * rows, lanes),
        vmem(2, 2, rows + 4, 2, count, lanes),
        pltpu.VMEM((2 * count, 10 * rows * lanes), jnp.bfloat16), pltpu.VMEM((4 * count, 10 * rows * lanes), jnp.bfloat16),

        pltpu.VMEM((4 * count, 4 * (rows + 3) * lanes), jnp.bfloat16), vmem(2 * count, rows * lanes),
        vmem(2, PAIR, lanes), vmem(2, PAIR * n_gx * n_gy, lanes),
        sem((9,)), sem((9,)), sem((2,)), sem((2,)), sem((7,)),
        pltpu.SemaphoreType.REGULAR((max(rounds_of(n_gy), 1),)),
    ]
    return pl.pallas_call(
        functools.partial(kernel, sizes),
        out_shape=pltpu.VMEM(probes.shape, jnp.float32),
        in_specs=[pl.BlockSpec(memory_space=pltpu.HBM)] * 7,
        out_specs=pl.BlockSpec(memory_space=pltpu.VMEM),
        scratch_shapes=scratch,
        compiler_params=pltpu.CompilerParams(collective_id=0, has_side_effects=True),
        name="hessian_probe",
    )(velocity, thickness, log_friction, obs_weight, ice_mask, grounded, probes)


def solution(mesh):
    sizes = (mesh.shape["gx"], mesh.shape["gy"])
    in_specs = (
        P(None, None, "gx", "gy"),
        P("gx", "gy"),
        P("gx", "gy"),
        P("gx", "gy"),
        P("gx", "gy"),
        P("gx", "gy"),
        P(None, "gx", "gy"),
    )
    out_specs = P(None, "gx", "gy")
    return jax.shard_map(
        functools.partial(body, sizes), mesh=mesh, in_specs=in_specs, out_specs=out_specs, check_vma=False
    )
```

```python
import functools

import jax
import jax.numpy as jnp
from jax import lax
from jax.experimental import pallas as pl
from jax.experimental.pallas import tpu as pltpu
from jax.sharding import PartitionSpec as P

MASS_TERM = 0.1
STRAIN_OFFSET = 0.01
ANISO_X = (4.0, 1.0)
ANISO_Y = (1.0, 4.0)
HIGHEST = lax.Precision.HIGHEST
MESH = pl.DeviceIdType.MESH
PAIR = 2
REACH = 5
SLOT = 2 * REACH
WEST, EAST, SOUTH, NORTH = range(4)
DIRS = range(4)
FORMS = 4


def rounds_of(count):
    rounds = 0
    while 2 ** (rounds + 1) < count - 1:
        rounds += 1
    return rounds


class Field:
    def __init__(self, tiles):
        self.tiles = tiles

    def _with(self, other, op):
        if isinstance(other, Field):
            return Field([None if a is None or b is None else op(a, b) for a, b in zip(self.tiles, other.tiles)])
        return Field([None if a is None else op(a, other) for a in self.tiles])

    def __add__(self, other):
        return self._with(other, lambda a, b: a + b)

    def __sub__(self, other):
        return self._with(other, lambda a, b: a - b)

    def __mul__(self, other):
        return self._with(other, lambda a, b: a * b)

    __radd__ = __add__
    __rmul__ = __mul__

    def map(self, op):
        return Field([None if a is None else op(a) for a in self.tiles])


def kernel(
    sizes,
    vel_hbm, thick_hbm, logf_hbm, obs_hbm, ice_hbm, ground_hbm, probes_hbm,
    out_ref,
    vel_ref, thick_ref, logf_ref, obs_ref, ice_ref, ground_ref, probes_ref,
    row, hrow, tn, ts, edge_src, edge_dst,
    coef, kzs, ratio, inverse, green, kept_ref, quad, drv, wmx, probe_strip,
    bx, left_0, right_0, left_1, right_1, results, mixed, tile_0, tile_1, landed_0, landed_1,
    send_sem, recv_sem, ar_send, ar_recv, in_sem, greet_sem,
):
    n_gx, n_gy = sizes
    lefts, rights, tile_src, landed = (left_0, left_1), (right_0, right_1), (tile_0, tile_1), (landed_0, landed_1)
    loads = [
        pltpu.make_async_copy(src, dst, in_sem.at[k])
        for k, (src, dst) in enumerate((
            (vel_hbm, vel_ref), (probes_hbm, probes_ref), (thick_hbm, thick_ref), (logf_hbm, logf_ref),
            (obs_hbm, obs_ref), (ice_hbm, ice_ref), (ground_hbm, ground_ref),
        ))
    ]
    for copy in loads:
        copy.start()
    layers = vel_ref.shape[1]
    rows = vel_ref.shape[2]
    lanes = vel_ref.shape[3]
    probes = probes_ref.shape[0]
    last = layers - 1
    half = rows // 2
    per_tile = layers + 1
    n_fields = 2 * per_tile + probes + 2
    ix = lax.axis_index("gx")
    iy = lax.axis_index("gy")
    tile = (rows, lanes)
    lane = lax.broadcasted_iota(jnp.int32, tile, 1)
    sub = lax.broadcasted_iota(jnp.int32, tile, 0)
    lane_first = lane == 0
    lane_last = lane == lanes - 1
    sub_first = sub == 0
    sub_last = sub == rows - 1
    slot_id = lane // SLOT
    high = lane - slot_id * SLOT < REACH

    barrier = pltpu.get_barrier_semaphore()
    peers = [
        {"gx": lax.rem(ix + step // n_gy, n_gx), "gy": lax.rem(iy + step % n_gy, n_gy)} for step in range(1, n_gx * n_gy)
    ]
    def lane_roll(t, shift):
        shift = shift % lanes
        return t if shift == 0 else pltpu.roll(t, shift, 1)

    def sub_roll(t, shift):
        return pltpu.roll(t, shift % rows, 0)

    def inside(dx, dy):
        tests = []
        if dx:
            tests.append(ix >= -dx if dx < 0 else ix < n_gx - dx)
        if dy:
            tests.append(iy >= -dy if dy < 0 else iy < n_gy - dy)
        return functools.reduce(jnp.logical_and, tests)

    def transfer(k, dx, dy, src, dst):
        target = {}
        if dx:
            target["gx"] = ix + dx
        if dy:
            target["gy"] = iy + dy
        copy = pltpu.make_async_remote_copy(
            src_ref=src, dst_ref=dst, send_sem=send_sem.at[k], recv_sem=recv_sem.at[k],
            device_id=target, device_id_type=MESH,
        )
        return copy, dst, inside(dx, dy), inside(-dx, -dy)

    for dy in (0, -1, 1, -2, 2):
        for step in range(n_gx):
            if step == 0 and dy == 0:
                continue
            target = {"gx": lax.rem(ix + step, n_gx), "gy": iy + dy}
            if dy == 0:
                pl.semaphore_signal(barrier, inc=1, device_id=target, device_id_type=MESH)
            else:
                @pl.when(inside(0, dy))
                def _(target=target):
                    pl.semaphore_signal(barrier, inc=1, device_id=target, device_id_type=MESH)
    low, top = pl.ds(0, half), pl.ds(half, half)
    corner_low, corner_top = pl.ds(rows, half), pl.ds(rows + half, half)
    own_pack = pl.ds(n_fields, 3)
    whole = pl.ds(0, rows)
    everything = pl.ds(0, n_fields + 3)
    packs = pl.ds(0, 3)
    exchange = [
        transfer(0, -1, 0, row.at[everything, low], hrow.at[everything, low]),
        transfer(1, 1, 0, row.at[everything, top], hrow.at[everything, top]),
        transfer(2, 0, -1, row.at[own_pack, whole], tn.at[packs, whole]),
        transfer(3, 0, 1, row.at[own_pack, whole], ts.at[packs, whole]),
        transfer(4, -1, -1, row.at[own_pack, low], tn.at[packs, corner_low]),
        transfer(5, 1, -1, row.at[own_pack, top], tn.at[packs, corner_top]),
        transfer(6, -1, 1, row.at[own_pack, low], ts.at[packs, corner_low]),
        transfer(7, 1, 1, row.at[own_pack, top], ts.at[packs, corner_top]),
    ]
    ahead, behind = pl.ds(0, 2), pl.ds(2, 1)
    edges = [
        transfer(8, -1, 0, edge_src.at[ahead], edge_dst.at[ahead]),
        transfer(9, 1, 0, edge_src.at[behind], edge_dst.at[behind]),
    ]

    for copy in loads:
        copy.wait()
    mask_own = ice_ref[...].astype(jnp.float32)
    friction_own = mask_own * ground_ref[...].astype(jnp.float32) * jnp.exp(logf_ref[...])
    wm_own = obs_ref[...] * mask_own
    own = [vel_ref[0, l] for l in range(layers)] + [thick_ref[...]]
    own += [vel_ref[1, l] for l in range(layers)] + [mask_own]
    own += [probes_ref[p] for p in range(probes)] + [friction_own, wm_own]
    for f, t in enumerate(own):
        row[f] = t
    for k in range(3):
        packed = None
        for s, t in enumerate(own[k * per_tile : (k + 1) * per_tile]):
            moved = lane_roll(t, s * SLOT + REACH)
            packed = moved if packed is None else jnp.where(slot_id == s, moved, packed)
        row[n_fields + k] = packed

    for _, dst, _, has_src in exchange + edges:
        @pl.when(jnp.logical_not(has_src))
        def _(dst=dst):
            dst[...] = jnp.zeros(dst.shape, jnp.float32)
    within = sum(inside(0, dy).astype(jnp.int32) for dy in (-1, 1, -2, 2)) + 1
    pl.semaphore_wait(barrier, n_gx * within - 1)
    for copy, _, has_dst, _ in exchange:
        pl.when(has_dst)(copy.start)

    def greet(k):
        for dy in (-(2 ** (k + 1)), 2 ** (k + 1)):
            @pl.when(inside(0, dy))
            def _(dy=dy):
                pl.semaphore_signal(greet_sem.at[k], inc=1, device_id={"gy": iy + dy}, device_id_type=MESH)

    def meet(k):
        if k < rounds:
            reach = 2 ** (k + 1)
            pl.semaphore_wait(
                greet_sem.at[k], inside(0, -reach).astype(jnp.int32) + inside(0, reach).astype(jnp.int32)
            )
        if k + 1 < rounds:
            greet(k + 1)

    rounds = rounds_of(n_gy)
    if rounds:
        greet(0)
    meet(0)
    for copy, _, _, has_src in exchange:
        pl.when(has_src)(copy.wait_recv)

    def shifted(f, axis, forward):
        if axis == 0:
            at, move, pairs = (sub_first, -1, ((0, 1), (1, 0), (2, 3), (3, 2))) if forward else (sub_last, 1, ((0, 1), (1, 0), (2, 3), (3, 2)))
            roll = sub_roll
        else:
            at, move, pairs = (lane_first, -1, ((0, 2), (1, 3), (2, 0), (3, 1))) if forward else (lane_last, 1, ((0, 2), (1, 3), (2, 0), (3, 1)))
            roll = lane_roll
        tiles = [None] * 4
        for a, b in pairs:
            if f.tiles[a] is not None and f.tiles[b] is not None:
                tiles[a] = roll(jnp.where(at, f.tiles[b], f.tiles[a]), move)
        return Field(tiles)

    def neighbour(f, d):
        return shifted(f, 0 if d in (WEST, EAST) else 1, d in (EAST, NORTH))

    both_packs = [
        [jnp.where(high, ts[k, pl.ds(h * rows, rows), :], tn[k, pl.ds(h * rows, rows), :]) for h in range(2)]
        for k in range(3)
    ]

    def strip(packs_of, s):
        return [lane_roll(t, -(s * SLOT + REACH)) for t in packs_of]

    def assemble(f):
        return Field([own[f], hrow[f]] + strip(both_packs[f // per_tile], f % per_tile))

    thick = assemble(layers).map(lambda t: jnp.where(t > 0.0, t, 1.0))
    inverse_step = thick.map(lambda t: last / t)
    mask = assemble(per_tile + layers)
    friction = assemble(2 * per_tile + probes)
    wm = assemble(2 * per_tile + probes + 1)

    def viscosity(ux, uy, uz, vx, vy, vz):
        shear = uy + vx
        strain = ux * ux + vy * vy + ux * vy + 0.25 * (shear * shear) + 0.25 * (uz * uz + vz * vz) + STRAIN_OFFSET
        root = jnp.exp(jnp.log(strain) * (-1.0 / 3.0))
        root = root + root * (1.0 - strain * root * root * root) * (1.0 / 3.0)
        return 0.5 * root

    strips = []
    for north_side in (True, False):
        def side(k):
            tiles = []
            for h in range(2):
                mine = row[n_fields + k] if h == 0 else hrow[n_fields + k]
                theirs = (tn if north_side else ts)[k, pl.ds(h * rows, rows), :]
                tiles.append(jnp.where(high, mine, theirs) if north_side else jnp.where(high, theirs, mine))
            return tiles
        u_side, v_side = side(0), side(1)
        steps = []
        for t in u_side:
            t = jnp.where(t > 0.0, t, 1.0)
            have = 1
            while have < per_tile:
                t = jnp.where(slot_id >= per_tile - have, t, lane_roll(t, -SLOT * have))
                have *= 2
            steps.append((0.5 * last) / t)
        mu = []
        grads = []
        for pair in (u_side, v_side):
            e = [sub_roll(jnp.where(sub_first, pair[1 - h], pair[h]), -1) for h in range(2)]
            w = [sub_roll(jnp.where(sub_last, pair[1 - h], pair[h]), 1) for h in range(2)]
            for h in range(2):
                t = pair[h]
                n, s = lane_roll(t, -1), lane_roll(t, 1)
                above = jnp.where(slot_id == last, t, lane_roll(t, -SLOT))
                below = jnp.where(slot_id == 0, t, lane_roll(t, SLOT))
                grads.append((0.5 * (e[h] - w[h]), 0.5 * (n - s), (above - below) * steps[h]))
        for h in range(2):
            mu.append(viscosity(*grads[h], *grads[2 + h]))
        strips.append(mu)
    mu_packs = [jnp.where(high, strips[1][h], strips[0][h]) for h in range(2)]

    half_step = Field((0.5 * inverse_step).tiles[:2] + [None, None])
    velocity = []
    for c in range(2):
        for l in range(layers):
            velocity.append(assemble(c * per_tile + l))
    visc = []
    for l in range(layers):
        grads = []
        for c in range(2):
            f = velocity[c * layers + l]
            main = Field(f.tiles[:2] + [None, None])
            gx = 0.5 * (neighbour(main, EAST) - neighbour(main, WEST))
            gy = 0.5 * (neighbour(f, NORTH) - neighbour(f, SOUTH))
            gz = (velocity[c * layers + min(l + 1, last)] - velocity[c * layers + max(l - 1, 0)]) * half_step
            grads.append((gx, gy, gz))
        (ux, uy, uz), (vx, vy, vz) = grads
        tiles = [
            viscosity(ux.tiles[h], uy.tiles[h], uz.tiles[h], vx.tiles[h], vy.tiles[h], vz.tiles[h]) for h in range(2)
        ]
        visc.append(Field(tiles + strip(mu_packs, l)))

    def store(ref, index, f):
        for k, t in enumerate(f.tiles):
            if t is not None:
                ref[index + (k,)] = t

    def load(ref, index, count=4):
        return Field([ref[index + (k,)] if k < count else None for k in range(4)])

    def scale_of(c, d):
        return ANISO_X[c] if d in (WEST, EAST) else ANISO_Y[c]

    for c in range(2):
        store(drv, (c,), friction * velocity[c * layers])
    store(wmx, (), wm)
    for p in range(probes):
        for h, t in enumerate(strip(both_packs[2], p)):
            probe_strip[p, pl.ds(h * rows, rows), :] = t

    mask_e = 0.5 * (mask * neighbour(mask, EAST))
    mask_n = 0.5 * (mask * neighbour(mask, NORTH))
    step2 = 0.5 * (inverse_step * inverse_step * mask)
    diag = MASS_TERM * mask + mask.map(lambda t: 1.0 - t)
    for l in range(layers):
        mu = visc[l]
        k_e = (mu + neighbour(mu, EAST)) * mask_e
        k_n = (mu + neighbour(mu, NORTH)) * mask_n
        for d, f in ((WEST, neighbour(k_e, WEST)), (EAST, k_e), (SOUTH, neighbour(k_n, SOUTH)), (NORTH, k_n)):
            for c in range(2):
                store(coef, (c, d, l), f if scale_of(c, d) == 1.0 else scale_of(c, d) * f)
        if l < last:
            store(kzs, (l,), (mu + visc[l + 1]) * step2)

    for c in range(2):
        ratios, inverses = [], []
        for l in range(layers):
            k = [load(coef, (c, d, l)) for d in DIRS]
            pivot = (k[WEST] + k[EAST]) + (k[SOUTH] + k[NORTH]) + diag
            if l == 0:
                pivot = pivot + friction
            if l > 0:
                below = load(kzs, (l - 1,))
                pivot = pivot + below
            if l < last:
                pivot = pivot + load(kzs, (l,))
            if l > 0:
                pivot = pivot - below * ratios[-1]
            inv = pivot.map(lambda t: 1.0 / t)
            inverses.append(inv)
            store(inverse, (c, l), inv)
            if l < last:
                ratios.append(load(kzs, (l,)) * inv)
                store(ratio, (c, l), ratios[-1])
        up = [inverses[0]]
        for l in range(1, layers):
            up.append(load(kzs, (l - 1,)) * up[-1] * inverses[l])
        from_bottom, from_top = up[last], inverses[last]
        for l in range(last, -1, -1):
            if l < last:
                from_bottom = up[l] + ratios[l] * from_bottom
                from_top = ratios[l] * from_top
            store(green, (0, c, l), from_bottom)
            store(green, (1, c, l), from_top)

    def prepare(p):
        src, kept = (0, last) if p == 0 else (last, 0)
        for c in range(2):
            quad[p, c, 0] = green[p, c, src, 0]
            cross = {}
            ys = []
            for l in range(layers):
                g = load(green, (p, c, l))
                inv = load(inverse, (c, l), 3)
                f = [load(coef, (c, d, l), 3) * neighbour(g, d) for d in DIRS]
                if l > 0:
                    below = load(kzs, (l - 1,), 3)
                    f = [f[d] + below * ys[-1][d] for d in DIRS]
                ys.append([f[d] * inv for d in DIRS])
                for d in DIRS:
                    for e in range(d, 4):
                        term = f[d].tiles[0] * ys[-1][e].tiles[0]
                        cross[d, e] = cross[d, e] + term if l > 0 else term
            at = 1 + len(DIRS)
            for term in cross.values():
                quad[p, c, at] = term
                at += 1
            x = ys[last]
            total = [[None] * 6 for _ in DIRS]
            for l in range(last, -1, -1):
                if l < last:
                    r = load(ratio, (c, l), 3)
                    x = [ys[l][d] + r * x[d] for d in DIRS]
                if l == kept:
                    for d in DIRS:
                        for k in (0, 2):
                            kept_ref[p, c, d, k] = x[d].tiles[k]
                if l == src:
                    for d in DIRS:
                        quad[p, c, 1 + d] = x[d].tiles[0]
                he = [sub_roll(jnp.where(sub_first, x[e].tiles[1], x[e].tiles[0]), -1) for e in DIRS]
                hn = [lane_roll(jnp.where(lane_first, x[e].tiles[2], x[e].tiles[0]), -1) for e in DIRS]
                k_e, k_n = coef[c, EAST, l, 0], coef[c, NORTH, l, 0]
                for d in DIRS:
                    t_e, t_n = k_e * x[d].tiles[0], k_n * x[d].tiles[0]
                    terms = [
                        t_e * he[WEST] + t_n * hn[SOUTH], t_e * he[EAST], t_e * he[SOUTH],
                        t_e * he[NORTH] + t_n * hn[EAST], t_n * hn[WEST], t_n * hn[NORTH],
                    ]
                    total[d] = [v if u is None else u + v for u, v in zip(total[d], terms)]
            for d in DIRS:
                for k in range(6):
                    quad[p, c, at] = total[d][k]
                    at += 1

    def where_row(r):
        return (0, r) if 0 <= r < rows else (1, r % rows)

    def main_strip(ref, index, r):
        h, at = where_row(r)
        return ref[index + (h, pl.ds(at, 1), slice(None))], ref[index + (2 + h, pl.ds(at, 1), slice(None))]

    def north_of(m, s):
        return lane_roll(jnp.where(lane_first, s, m), -1)

    def south_of(m, s):
        return lane_roll(jnp.where(lane_last, s, m), 1)

    def b_of(p, c, r, s=0):
        return bx[p, c, r + 2, s]

    def remainder(t):
        return t - t.astype(jnp.bfloat16).astype(jnp.float32)

    def halves(t):
        return jnp.concatenate([t, remainder(t)], axis=0).astype(jnp.bfloat16)

    def at_k(block, c, i):
        return pl.ds(((block * 2 + c) * rows + i) * lanes, lanes)

    def bases_of(p):
        return (0,) if p == 0 else (1, 2)

    def put_left(p, block, c, i, parts):
        if p == 0:
            lefts[p][:, at_k(block, c, i)] = halves(parts[0])
        else:
            t = jnp.concatenate(parts, axis=0)
            lefts[p][0 : 2 * probes, at_k(block, c, i)] = t.astype(jnp.bfloat16)
            lefts[p][2 * probes :, at_k(block, c, i)] = remainder(t).astype(jnp.bfloat16)

    def put_right(p, block, c, i, one, two):
        step = 2 * probes
        both = one + two
        groups = [jnp.concatenate(both[n : n + 2], axis=0) for n in range(0, len(both), 2)]
        for n, t in enumerate(groups):
            rights[p][n * step : (n + 1) * step, at_k(block, c, i)] = t.astype(jnp.bfloat16)
            m = n + len(groups)
            rights[p][m * step : (m + 1) * step, at_k(block, c, i)] = remainder(t).astype(jnp.bfloat16)

    def tree(terms):
        while len(terms) > 1:
            terms = [terms[n] + terms[n + 1] if n + 1 < len(terms) else terms[n] for n in range(0, len(terms), 2)]
        return terms[0]

    def stencil_row(p, c, i):
        q = quad.at[p, c]

        def row_of(index):
            return q[index, pl.ds(i, 1), :]

        count = 1 + len(DIRS)
        cross = {}
        for d in DIRS:
            for e in range(d, 4):
                cross[d, e] = cross[e, d] = row_of(count)
                count += 1
        ones, twos, arounds, centres = [[] for _ in range(5)], [[] for _ in range(5)], [], []
        for n in bases_of(p):
            b0 = b_of(n, c, i)
            n_w, n_0, n_e = (north_of(b_of(n, c, i + d), b_of(n, c, i + d, 1)) for d in (-1, 0, 1))
            s_0, s_e = (south_of(b_of(n, c, i + d), b_of(n, c, i + d, 1)) for d in (0, 1))
            n_2 = lane_roll(jnp.where(lane < 2, b_of(n, c, i, 1), b0), -2)
            around = [b_of(n, c, i - 1), b_of(n, c, i + 1), s_0, n_0]
            far = [b0, b_of(n, c, i + 2), s_e, n_e, n_w, n_2]
            centres.append(b0)
            arounds.append(around)
            ones[0].append(row_of(0) * b0)
            twos[0].append(tree([row_of(1 + d) * around[d] for d in DIRS]))
            for d in DIRS:
                ones[1 + d].append(tree([cross[d, e] * around[e] for e in DIRS]))
                twos[1 + d].append(tree([row_of(count + 6 * d + j) * far[j] for j in range(6)]))
        put_left(p, 0, c, i, centres)
        for d in DIRS:
            put_left(p, 1 + d, c, i, [around[d] for around in arounds])
        for block in range(5):
            put_right(p, block, c, i, ones[block], twos[block])

    def contract(p):
        cut = 2 * rows * lanes
        size = probes * len(bases_of(p))
        results = []
        for at, span in ((0, cut), (cut, 4 * cut)):
            both = lax.dot_general(
                lefts[p][:, pl.ds(at, span)], rights[p][:, pl.ds(at, span)], (((1,), (1,)), ((), ())),
                preferred_element_type=jnp.float32,
            )
            both = both[0:size, :] + both[size:, :]
            results.append(both[:, 0 : 2 * size] + both[:, 2 * size :])
        return jnp.concatenate(results, axis=1)

    width = FORMS * probes

    def start_sum(p, tile_rows, packed):
        mine = pl.ds((ix * n_gy + iy) * tile_rows, tile_rows)
        landed[p][mine, :] = packed
        tile_src[p][...] = packed
        for peer in peers:
            pltpu.make_async_remote_copy(
                src_ref=tile_src[p], dst_ref=landed[p].at[mine], send_sem=ar_send.at[p], recv_sem=ar_recv.at[p],
                device_id=peer, device_id_type=MESH,
            ).start()

    def everyone(p):
        total_rows = pl.ds(0, (PAIR, rows)[p] * len(peers))
        return pltpu.make_async_remote_copy(
            src_ref=landed[p].at[total_rows], dst_ref=landed[p].at[total_rows], send_sem=ar_send.at[p],
            recv_sem=ar_recv.at[p], device_id=peers[0], device_id_type=MESH,
        )

    def start_first():
        grams = jnp.concatenate([contract(0), jnp.zeros((probes, lanes - width), jnp.float32)], axis=1)
        packed = grams
        for q in range(1, probes // PAIR):
            packed = jnp.where(lane < q * width, packed, lane_roll(sub_roll(grams, -PAIR * q), q * width))
        start_sum(0, PAIR, packed[0:PAIR, :])

    def start_second():
        forms = contract(1)
        start_sum(1, rows, jnp.concatenate([forms[0:probes, :], forms[probes:, :]], axis=1))

    def landed_sum(p):
        return tree([landed[p][k * probes : (k + 1) * probes, :] for k in range(landed[p].shape[0] // probes)])

    def first_grams():
        packed = landed_sum(0)
        shift = PAIR
        while shift < probes:
            packed = packed + sub_roll(packed, shift)
            shift *= 2
        grams = packed
        for q in range(1, probes // PAIR):
            grams = jnp.where(sub < PAIR * q, grams, lane_roll(packed, -q * width))
        return grams

    def dot(a, b, dims):
        return lax.dot_general(a, b, (dims, ((), ())), precision=HIGHEST, preferred_element_type=jnp.float32)

    def second_grams(mixing):
        forms = landed_sum(1)
        size = 2 * probes
        forms = jnp.concatenate([forms[:, 0 : FORMS * size], forms[:, FORMS * size :]], axis=0)
        half_mixed = dot(mixing, forms, ((1,), (0,)))
        stacked = jnp.concatenate([half_mixed[:, f * size : (f + 1) * size] for f in range(FORMS)], axis=0)
        full = dot(stacked, mixing, ((1,), (1,)))
        parts = [full[f * probes : (f + 1) * probes, :] for f in range(FORMS)]
        return jnp.concatenate(parts + [jnp.zeros((probes, lanes - width), jnp.float32)], axis=1)

    def mixing_of(grams):
        base = (FORMS - 1) * probes
        mirrored = grams
        for r in range(probes):
            column = jnp.sum(
                jnp.where(lane == base + sub, jnp.broadcast_to(grams[r : r + 1, :], tile), 0.0), axis=1, keepdims=True
            )
            mirrored = jnp.where(lane == base + r, grams + column, mirrored)
        grams = mirrored
        diff = grams - lane_roll(grams, -probes)
        upper = jnp.where(lane < 2 * probes, diff, lane_roll(grams, 2 * probes))
        lower = jnp.where(lane < 2 * probes, lane_roll(diff, -probes), lane_roll(grams, probes))
        size = 2 * probes
        both = [upper, lower]
        scale = [jnp.sum(jnp.where(lane == sub + h * probes, both[h], 0.0), axis=1, keepdims=True) for h in range(2)]
        for k in range(size):
            h, r = k // probes, k % probes
            line = both[h][r : r + 1, :]
            pivot = line[:, k : k + 1]
            inv = jnp.where(pivot > 1e-6 * scale[h][r : r + 1, :], 1.0 / pivot, 0.0)
            line = line * inv
            for q in range(2):
                updated = both[q] - both[q][:, k : k + 1] * line
                both[q] = jnp.where(sub == r, line, updated) if q == h else updated
        pick = (lane == sub + size).astype(jnp.float32)
        return dot(pick, jnp.concatenate(both, axis=0), ((1,), (1,)))

    prepare(0)
    for r in range(-2, rows + 2):
        h, at = where_row(r)
        main = probes_ref[:, at, :] if h == 0 else hrow[2 * per_tile : 2 * per_tile + probes, at, :]
        side = probe_strip[:, h * rows + at, :]
        for c in range(2):
            d_main, d_side = main_strip(drv, (c,), r)
            bx[0, c, r + 2, 0] = main * d_main
            bx[0, c, r + 2, 1] = side * d_side

    def surface(c, r):
        m, s = b_of(0, c, r), b_of(0, c, r, 1)
        sides = [
            (b_of(0, c, r - 1), b_of(0, c, r - 1, 1)), (b_of(0, c, r + 1), b_of(0, c, r + 1, 1)),
            (south_of(m, s), south_of(s, m)), (north_of(m, s), north_of(s, m)),
        ]
        hs = [main_strip(kept_ref, (0, c, d), r) for d in DIRS]
        return [tree([hs[d][k] * sides[d][k] for d in DIRS]) for k in range(2)]

    sent_rows = (0, 1, rows - 1)
    got_rows = (rows, rows + 1, -1)
    for n, r in enumerate(sent_rows):
        for c in range(2):
            x = surface(c, r)
            for k in range(2):
                edge_src[n, c, k] = x[k]
    for copy, _, has_dst, _ in edges:
        pl.when(has_dst)(copy.start)
    for c in range(2):
        for i in range(rows):
            stencil_row(0, c, i)
    for k in range(1, rounds):
        meet(k)
    start_first()
    prepare(1)

    def fill_row(c, r, x):
        g = main_strip(green, (0, c, last), r)
        w = main_strip(wmx, (), r)
        for k in range(2):
            bx[1, c, r + 2, k] = (g[k] * w[k]) * b_of(0, c, r, k)
            bx[2, c, r + 2, k] = w[k] * x[k]

    inner = range(1, rows - 2)
    for c in range(2):
        for r in range(rows):
            fill_row(c, r, [edge_src[sent_rows.index(r), c, k] for k in range(2)] if r in sent_rows else surface(c, r))
    for c in range(2):
        for i in inner:
            stencil_row(1, c, i)
    for copy, _, _, has_src in edges:
        pl.when(has_src)(copy.wait_recv)
    for n, r in enumerate(got_rows):
        for c in range(2):
            fill_row(c, r, [edge_dst[n, c, k] for k in range(2)])
    for c in range(2):
        for i in range(rows):
            if i not in inner:
                stencil_row(1, c, i)
    start_second()
    for i in range(rows):
        at = pl.ds(i * lanes, lanes)
        for n in bases_of(1):
            total = [None, None]
            for c in range(2):
                drive = drv[c, 0, pl.ds(i, 1), :]
                m, s = b_of(n, c, i), b_of(n, c, i, 1)
                around = [b_of(n, c, i - 1), b_of(n, c, i + 1), south_of(m, s), north_of(m, s)]
                parts = [
                    (drive * green[1, c, 0, 0, pl.ds(i, 1), :]) * m,
                    drive * tree([kept_ref[1, c, d, 0, pl.ds(i, 1), :] * around[d] for d in DIRS]),
                ]
                total = [b if a is None else a + b for a, b in zip(total, parts)]
            for k in range(2):
                results[k, (n - 1) * probes : n * probes, at] = total[k]
    everyone(0).wait_recv()
    mixing = mixing_of(first_grams())
    for k in range(2):
        mixed[k * probes : (k + 1) * probes, :] = dot(mixing, results[k], ((1,), (0,)))
    everyone(1).wait_recv()
    final = dot(mixing_of(second_grams(mixing)), mixed[...], ((1,), (0,)))
    for i in range(rows):
        out_ref[:, i, :] = final[:, i * lanes : (i + 1) * lanes]
    for copy, _, has_dst, _ in exchange + edges:
        pl.when(has_dst)(copy.wait_send)
    for p in range(2):
        everyone(p).wait_send()


def body(sizes, velocity, thickness, log_friction, obs_weight, ice_mask, grounded, probes):
    layers, rows, lanes = velocity.shape[1:]
    count = probes.shape[0]
    n_gx, n_gy = sizes
    fields = 2 * (layers + 1) + count + 2 + 3
    forms = 1 + 4 + 10 + 24

    def vmem(*shape):
        return pltpu.VMEM(shape, jnp.float32)

    def half(*shape):
        return pltpu.VMEM(shape, jnp.bfloat16)

    sem = pltpu.SemaphoreType.DMA
    scratch = [
        vmem(*velocity.shape), vmem(rows, lanes), vmem(rows, lanes), vmem(rows, lanes),
        pltpu.VMEM((rows, lanes), jnp.int32), pltpu.VMEM((rows, lanes), jnp.int32), vmem(*probes.shape),
        vmem(fields, rows, lanes), vmem(fields, rows, lanes), vmem(3, 2 * rows, lanes), vmem(3, 2 * rows, lanes),
        vmem(3, 2, 2, count, lanes), vmem(3, 2, 2, count, lanes),
        vmem(2, 4, layers, 4, rows, lanes), vmem(layers - 1, 4, rows, lanes), vmem(2, layers - 1, 4, rows, lanes),
        vmem(2, layers, 4, rows, lanes), vmem(2, 2, layers, 4, rows, lanes),
        vmem(2, 2, 4, 4, rows, lanes), vmem(2, 2, forms, rows, lanes),
        vmem(2, 4, rows, lanes), vmem(4, rows, lanes), vmem(count, 2 * rows, lanes),
        vmem(3, 2, rows + 4, 2, count, lanes),
        half(2 * count, 10 * rows * lanes), half(4 * count, 10 * rows * lanes),
        half(4 * count, 10 * rows * lanes), half(8 * count, 10 * rows * lanes),
        vmem(2, 2 * count, rows * lanes), vmem(2 * count, rows * lanes),
        vmem(PAIR, lanes), vmem(rows, lanes), vmem(PAIR * n_gx * n_gy, lanes), vmem(rows * n_gx * n_gy, lanes),
        sem((10,)), sem((10,)), sem((2,)), sem((2,)), sem((7,)),
        pltpu.SemaphoreType.REGULAR((max(rounds_of(n_gy), 1),)),
    ]
    return pl.pallas_call(
        functools.partial(kernel, sizes),
        out_shape=pltpu.VMEM(probes.shape, jnp.float32),
        in_specs=[pl.BlockSpec(memory_space=pltpu.HBM)] * 7,
        out_specs=pl.BlockSpec(memory_space=pltpu.VMEM),
        scratch_shapes=scratch,
        compiler_params=pltpu.CompilerParams(collective_id=0, has_side_effects=True),
        name="hessian_probe",
    )(velocity, thickness, log_friction, obs_weight, ice_mask, grounded, probes)


def solution(mesh):
    sizes = (mesh.shape["gx"], mesh.shape["gy"])
    in_specs = (
        P(None, None, "gx", "gy"),
        P("gx", "gy"),
        P("gx", "gy"),
        P("gx", "gy"),
        P("gx", "gy"),
        P("gx", "gy"),
        P(None, "gx", "gy"),
    )
    out_specs = P(None, "gx", "gy")
    return jax.shard_map(
        functools.partial(body, sizes), mesh=mesh, in_specs=in_specs, out_specs=out_specs, check_vma=False
    )
```

```python
import functools

import jax
import jax.numpy as jnp
from jax import lax
from jax.experimental import pallas as pl
from jax.experimental.pallas import tpu as pltpu
from jax.sharding import PartitionSpec as P

MASS_TERM = 0.1
STRAIN_OFFSET = 0.01
ANISO_X = (4.0, 1.0)
ANISO_Y = (1.0, 4.0)
HIGHEST = lax.Precision.HIGHEST
MESH = pl.DeviceIdType.MESH
PAIR = 2
REACH = 5
SLOT = 2 * REACH
WEST, EAST, SOUTH, NORTH = range(4)
DIRS = range(4)
FORMS = 4


def rounds_of(count):
    rounds = 0
    while 2 ** (rounds + 1) < count - 1:
        rounds += 1
    return rounds


class Field:
    def __init__(self, tiles):
        self.tiles = tiles

    def _with(self, other, op):
        if isinstance(other, Field):
            return Field([None if a is None or b is None else op(a, b) for a, b in zip(self.tiles, other.tiles)])
        return Field([None if a is None else op(a, other) for a in self.tiles])

    def __add__(self, other):
        return self._with(other, lambda a, b: a + b)

    def __sub__(self, other):
        return self._with(other, lambda a, b: a - b)

    def __mul__(self, other):
        return self._with(other, lambda a, b: a * b)

    __radd__ = __add__
    __rmul__ = __mul__

    def map(self, op):
        return Field([None if a is None else op(a) for a in self.tiles])


def kernel(
    sizes,
    vel_hbm, thick_hbm, logf_hbm, obs_hbm, ice_hbm, ground_hbm, probes_hbm,
    out_ref,
    vel_ref, thick_ref, logf_ref, obs_ref, ice_ref, ground_ref, probes_ref,
    row, hrow, tn, ts, edge_src, edge_dst,
    coef, kzs, ratio, inverse, green, kept_ref, quad, drv, wmx, probe_strip,
    bx, left_0, right_0, left_1, right_1, results, mixed, tile_0, tile_1, landed_0, landed_1,
    send_sem, recv_sem, ar_send, ar_recv, in_sem, greet_sem,
):
    n_gx, n_gy = sizes
    lefts, rights, tile_src, landed = (left_0, left_1), (right_0, right_1), (tile_0, tile_1), (landed_0, landed_1)
    loads = [
        pltpu.make_async_copy(src, dst, in_sem.at[k])
        for k, (src, dst) in enumerate((
            (vel_hbm, vel_ref), (probes_hbm, probes_ref), (thick_hbm, thick_ref), (logf_hbm, logf_ref),
            (obs_hbm, obs_ref), (ice_hbm, ice_ref), (ground_hbm, ground_ref),
        ))
    ]
    for copy in loads:
        copy.start()
    layers = vel_ref.shape[1]
    rows = vel_ref.shape[2]
    lanes = vel_ref.shape[3]
    probes = probes_ref.shape[0]
    last = layers - 1
    half = rows // 2
    per_tile = layers + 1
    n_fields = 2 * per_tile + probes + 2
    ix = lax.axis_index("gx")
    iy = lax.axis_index("gy")
    tile = (rows, lanes)
    lane = lax.broadcasted_iota(jnp.int32, tile, 1)
    sub = lax.broadcasted_iota(jnp.int32, tile, 0)
    lane_first = lane == 0
    lane_last = lane == lanes - 1
    sub_first = sub == 0
    sub_last = sub == rows - 1
    slot_id = lane // SLOT
    high = lane - slot_id * SLOT < REACH

    barrier = pltpu.get_barrier_semaphore()
    peers = [
        {"gx": lax.rem(ix + step // n_gy, n_gx), "gy": lax.rem(iy + step % n_gy, n_gy)} for step in range(1, n_gx * n_gy)
    ]
    def lane_roll(t, shift):
        shift = shift % lanes
        return t if shift == 0 else pltpu.roll(t, shift, 1)

    def sub_roll(t, shift):
        return pltpu.roll(t, shift % rows, 0)

    def inside(dx, dy):
        tests = []
        if dx:
            tests.append(ix >= -dx if dx < 0 else ix < n_gx - dx)
        if dy:
            tests.append(iy >= -dy if dy < 0 else iy < n_gy - dy)
        return functools.reduce(jnp.logical_and, tests)

    def transfer(k, dx, dy, src, dst):
        target = {}
        if dx:
            target["gx"] = ix + dx
        if dy:
            target["gy"] = iy + dy
        copy = pltpu.make_async_remote_copy(
            src_ref=src, dst_ref=dst, send_sem=send_sem.at[k], recv_sem=recv_sem.at[k],
            device_id=target, device_id_type=MESH,
        )
        return copy, dst, inside(dx, dy), inside(-dx, -dy)

    for dy in (0, -1, 1, -2, 2):
        for step in range(n_gx):
            if step == 0 and dy == 0:
                continue
            target = {"gx": lax.rem(ix + step, n_gx), "gy": iy + dy}
            if dy == 0:
                pl.semaphore_signal(barrier, inc=1, device_id=target, device_id_type=MESH)
            else:
                @pl.when(inside(0, dy))
                def _(target=target):
                    pl.semaphore_signal(barrier, inc=1, device_id=target, device_id_type=MESH)
    low, top = pl.ds(0, half), pl.ds(half, half)
    corner_low, corner_top = pl.ds(rows, half), pl.ds(rows + half, half)
    own_pack = pl.ds(n_fields, 3)
    whole = pl.ds(0, rows)
    everything = pl.ds(0, n_fields + 3)
    packs = pl.ds(0, 3)
    exchange = [
        transfer(0, -1, 0, row.at[everything, low], hrow.at[everything, low]),
        transfer(1, 1, 0, row.at[everything, top], hrow.at[everything, top]),
        transfer(2, 0, -1, row.at[own_pack, whole], tn.at[packs, whole]),
        transfer(3, 0, 1, row.at[own_pack, whole], ts.at[packs, whole]),
        transfer(4, -1, -1, row.at[own_pack, low], tn.at[packs, corner_low]),
        transfer(5, 1, -1, row.at[own_pack, top], tn.at[packs, corner_top]),
        transfer(6, -1, 1, row.at[own_pack, low], ts.at[packs, corner_low]),
        transfer(7, 1, 1, row.at[own_pack, top], ts.at[packs, corner_top]),
    ]
    ahead, behind = pl.ds(0, 2), pl.ds(2, 1)
    edges = [
        transfer(8, -1, 0, edge_src.at[ahead], edge_dst.at[ahead]),
        transfer(9, 1, 0, edge_src.at[behind], edge_dst.at[behind]),
    ]

    for copy in loads:
        copy.wait()
    mask_own = ice_ref[...].astype(jnp.float32)
    friction_own = mask_own * ground_ref[...].astype(jnp.float32) * jnp.exp(logf_ref[...])
    wm_own = obs_ref[...] * mask_own
    own = [vel_ref[0, l] for l in range(layers)] + [thick_ref[...]]
    own += [vel_ref[1, l] for l in range(layers)] + [mask_own]
    own += [probes_ref[p] for p in range(probes)] + [friction_own, wm_own]
    for f, t in enumerate(own):
        row[f] = t
    for k in range(3):
        packed = None
        for s, t in enumerate(own[k * per_tile : (k + 1) * per_tile]):
            moved = lane_roll(t, s * SLOT + REACH)
            packed = moved if packed is None else jnp.where(slot_id == s, moved, packed)
        row[n_fields + k] = packed

    within = sum(inside(0, dy).astype(jnp.int32) for dy in (-1, 1, -2, 2)) + 1
    pl.semaphore_wait(barrier, n_gx * within - 1)
    for copy, _, has_dst, _ in exchange:
        pl.when(has_dst)(copy.start)
    for _, dst, _, has_src in exchange + edges:
        @pl.when(jnp.logical_not(has_src))
        def _(dst=dst):
            dst[...] = jnp.zeros(dst.shape, jnp.float32)

    def greet(k):
        for dy in (-(2 ** (k + 1)), 2 ** (k + 1)):
            @pl.when(inside(0, dy))
            def _(dy=dy):
                pl.semaphore_signal(greet_sem.at[k], inc=1, device_id={"gy": iy + dy}, device_id_type=MESH)

    def meet(k):
        if k < rounds:
            reach = 2 ** (k + 1)
            pl.semaphore_wait(
                greet_sem.at[k], inside(0, -reach).astype(jnp.int32) + inside(0, reach).astype(jnp.int32)
            )
        if k + 1 < rounds:
            greet(k + 1)

    rounds = rounds_of(n_gy)
    if rounds:
        greet(0)
    meet(0)
    for copy, _, _, has_src in exchange:
        pl.when(has_src)(copy.wait_recv)

    def shifted(f, axis, forward):
        if axis == 0:
            at, move, pairs = (sub_first, -1, ((0, 1), (1, 0), (2, 3), (3, 2))) if forward else (sub_last, 1, ((0, 1), (1, 0), (2, 3), (3, 2)))
            roll = sub_roll
        else:
            at, move, pairs = (lane_first, -1, ((0, 2), (1, 3), (2, 0), (3, 1))) if forward else (lane_last, 1, ((0, 2), (1, 3), (2, 0), (3, 1)))
            roll = lane_roll
        tiles = [None] * 4
        for a, b in pairs:
            if f.tiles[a] is not None and f.tiles[b] is not None:
                tiles[a] = roll(jnp.where(at, f.tiles[b], f.tiles[a]), move)
        return Field(tiles)

    def neighbour(f, d):
        return shifted(f, 0 if d in (WEST, EAST) else 1, d in (EAST, NORTH))

    both_packs = [
        [jnp.where(high, ts[k, pl.ds(h * rows, rows), :], tn[k, pl.ds(h * rows, rows), :]) for h in range(2)]
        for k in range(3)
    ]

    def strip(packs_of, s):
        return [lane_roll(t, -(s * SLOT + REACH)) for t in packs_of]

    def assemble(f):
        return Field([own[f], hrow[f]] + strip(both_packs[f // per_tile], f % per_tile))

    thick = assemble(layers).map(lambda t: jnp.where(t > 0.0, t, 1.0))
    inverse_step = thick.map(lambda t: last / t)
    mask = assemble(per_tile + layers)
    friction = assemble(2 * per_tile + probes)
    wm = assemble(2 * per_tile + probes + 1)

    def viscosity(ux, uy, uz, vx, vy, vz):
        shear = uy + vx
        strain = ux * ux + vy * vy + ux * vy + 0.25 * (shear * shear) + 0.25 * (uz * uz + vz * vz) + STRAIN_OFFSET
        root = jnp.exp(jnp.log(strain) * (-1.0 / 3.0))
        root = root + root * (1.0 - strain * root * root * root) * (1.0 / 3.0)
        return 0.5 * root

    strips = []
    for north_side in (True, False):
        def side(k):
            tiles = []
            for h in range(2):
                mine = row[n_fields + k] if h == 0 else hrow[n_fields + k]
                theirs = (tn if north_side else ts)[k, pl.ds(h * rows, rows), :]
                tiles.append(jnp.where(high, mine, theirs) if north_side else jnp.where(high, theirs, mine))
            return tiles
        u_side, v_side = side(0), side(1)
        steps = []
        for t in u_side:
            t = jnp.where(t > 0.0, t, 1.0)
            have = 1
            while have < per_tile:
                t = jnp.where(slot_id >= per_tile - have, t, lane_roll(t, -SLOT * have))
                have *= 2
            steps.append((0.5 * last) / t)
        mu = []
        grads = []
        for pair in (u_side, v_side):
            e = [sub_roll(jnp.where(sub_first, pair[1 - h], pair[h]), -1) for h in range(2)]
            w = [sub_roll(jnp.where(sub_last, pair[1 - h], pair[h]), 1) for h in range(2)]
            for h in range(2):
                t = pair[h]
                n, s = lane_roll(t, -1), lane_roll(t, 1)
                above = jnp.where(slot_id == last, t, lane_roll(t, -SLOT))
                below = jnp.where(slot_id == 0, t, lane_roll(t, SLOT))
                grads.append((0.5 * (e[h] - w[h]), 0.5 * (n - s), (above - below) * steps[h]))
        for h in range(2):
            mu.append(viscosity(*grads[h], *grads[2 + h]))
        strips.append(mu)
    mu_packs = [jnp.where(high, strips[1][h], strips[0][h]) for h in range(2)]

    half_step = Field((0.5 * inverse_step).tiles[:2] + [None, None])
    velocity = []
    for c in range(2):
        for l in range(layers):
            velocity.append(assemble(c * per_tile + l))
    visc = []
    for l in range(layers):
        grads = []
        for c in range(2):
            f = velocity[c * layers + l]
            main = Field(f.tiles[:2] + [None, None])
            gx = 0.5 * (neighbour(main, EAST) - neighbour(main, WEST))
            gy = 0.5 * (neighbour(f, NORTH) - neighbour(f, SOUTH))
            gz = (velocity[c * layers + min(l + 1, last)] - velocity[c * layers + max(l - 1, 0)]) * half_step
            grads.append((gx, gy, gz))
        (ux, uy, uz), (vx, vy, vz) = grads
        tiles = [
            viscosity(ux.tiles[h], uy.tiles[h], uz.tiles[h], vx.tiles[h], vy.tiles[h], vz.tiles[h]) for h in range(2)
        ]
        visc.append(Field(tiles + strip(mu_packs, l)))

    def store(ref, index, f):
        for k, t in enumerate(f.tiles):
            if t is not None:
                ref[index + (k,)] = t

    def load(ref, index, count=4):
        return Field([ref[index + (k,)] if k < count else None for k in range(4)])

    def scale_of(c, d):
        return ANISO_X[c] if d in (WEST, EAST) else ANISO_Y[c]

    for c in range(2):
        store(drv, (c,), friction * velocity[c * layers])
    store(wmx, (), wm)
    for p in range(probes):
        for h, t in enumerate(strip(both_packs[2], p)):
            probe_strip[p, pl.ds(h * rows, rows), :] = t

    mask_e = 0.5 * (mask * neighbour(mask, EAST))
    mask_n = 0.5 * (mask * neighbour(mask, NORTH))
    step2 = 0.5 * (inverse_step * inverse_step * mask)
    diag = MASS_TERM * mask + mask.map(lambda t: 1.0 - t)
    for l in range(layers):
        mu = visc[l]
        k_e = (mu + neighbour(mu, EAST)) * mask_e
        k_n = (mu + neighbour(mu, NORTH)) * mask_n
        for d, f in ((WEST, neighbour(k_e, WEST)), (EAST, k_e), (SOUTH, neighbour(k_n, SOUTH)), (NORTH, k_n)):
            for c in range(2):
                store(coef, (c, d, l), f if scale_of(c, d) == 1.0 else scale_of(c, d) * f)
        if l < last:
            store(kzs, (l,), (mu + visc[l + 1]) * step2)

    for c in range(2):
        ratios, inverses = [], []
        for l in range(layers):
            k = [load(coef, (c, d, l)) for d in DIRS]
            pivot = (k[WEST] + k[EAST]) + (k[SOUTH] + k[NORTH]) + diag
            if l == 0:
                pivot = pivot + friction
            if l > 0:
                below = load(kzs, (l - 1,))
                pivot = pivot + below
            if l < last:
                pivot = pivot + load(kzs, (l,))
            if l > 0:
                pivot = pivot - below * ratios[-1]
            inv = pivot.map(lambda t: 1.0 / t)
            inverses.append(inv)
            store(inverse, (c, l), inv)
            if l < last:
                ratios.append(load(kzs, (l,)) * inv)
                store(ratio, (c, l), ratios[-1])
        up = [inverses[0]]
        for l in range(1, layers):
            up.append(load(kzs, (l - 1,)) * up[-1] * inverses[l])
        from_bottom, from_top = up[last], inverses[last]
        for l in range(last, -1, -1):
            if l < last:
                from_bottom = up[l] + ratios[l] * from_bottom
                from_top = ratios[l] * from_top
            store(green, (0, c, l), from_bottom)
            store(green, (1, c, l), from_top)

    def prepare(p, between=lambda: None):
        src, kept = (0, last) if p == 0 else (last, 0)
        for c in range(2):
            quad[p, c, 0] = 0.5 * green[p, c, src, 0]
            cross = {}
            ys = []
            for l in range(layers):
                g = load(green, (p, c, l))
                inv = load(inverse, (c, l), 3)
                f = [load(coef, (c, d, l), 3) * neighbour(g, d) for d in DIRS]
                if l > 0:
                    below = load(kzs, (l - 1,), 3)
                    f = [f[d] + below * ys[-1][d] for d in DIRS]
                ys.append([f[d] * inv for d in DIRS])
                between()
                for d in DIRS:
                    for e in range(d, 4):
                        term = f[d].tiles[0] * ys[-1][e].tiles[0]
                        cross[d, e] = cross[d, e] + term if l > 0 else term
            at = 3
            for (d, e), term in cross.items():
                quad[p, c, at] = 0.5 * term if d == e else term
                at += 1
            x = ys[last]
            total = [[None] * 6 for _ in DIRS]
            for l in range(last, -1, -1):
                if l < last:
                    r = load(ratio, (c, l), 3)
                    x = [ys[l][d] + r * x[d] for d in DIRS]
                between()
                if l == kept:
                    for d in DIRS:
                        for k in (0, 2):
                            kept_ref[p, c, d, k] = x[d].tiles[k]
                if l == src:
                    quad[p, c, 1] = x[EAST].tiles[0]
                    quad[p, c, 2] = x[NORTH].tiles[0]
                he = [sub_roll(jnp.where(sub_first, x[e].tiles[1], x[e].tiles[0]), -1) for e in DIRS]
                hn = [lane_roll(jnp.where(lane_first, x[e].tiles[2], x[e].tiles[0]), -1) for e in DIRS]
                k_e, k_n = coef[c, EAST, l, 0], coef[c, NORTH, l, 0]
                for d in DIRS:
                    t_e, t_n = k_e * x[d].tiles[0], k_n * x[d].tiles[0]
                    terms = [
                        t_e * he[WEST] + t_n * hn[SOUTH], t_e * he[EAST], t_e * he[SOUTH],
                        t_e * he[NORTH] + t_n * hn[EAST], t_n * hn[WEST], t_n * hn[NORTH],
                    ]
                    total[d] = [v if u is None else u + v for u, v in zip(total[d], terms)]
            for d in DIRS:
                for k in range(6):
                    quad[p, c, at] = total[d][k]
                    at += 1

    def where_row(r):
        return (0, r) if 0 <= r < rows else (1, r % rows)

    def main_strip(ref, index, r):
        h, at = where_row(r)
        return ref[index + (h, pl.ds(at, 1), slice(None))], ref[index + (2 + h, pl.ds(at, 1), slice(None))]

    def north_of(m, s):
        return lane_roll(jnp.where(lane_first, s, m), -1)

    def south_of(m, s):
        return lane_roll(jnp.where(lane_last, s, m), 1)

    def b_of(p, c, r, s=0):
        return bx[p, c, r + 2, s]

    def split(t):
        head = t.astype(jnp.bfloat16)
        return head, (t - head.astype(jnp.float32)).astype(jnp.bfloat16)

    def halves(t):
        return jnp.concatenate([t, t - t.astype(jnp.bfloat16).astype(jnp.float32)], axis=0).astype(jnp.bfloat16)

    inner = list(range(1, rows - 2))
    outer = [i for i in range(rows) if i not in inner]
    cut = 10 * len(inner)

    def at_k(block, c, i):
        group = inner if i in inner else outer
        base = 0 if i in inner else cut
        return pl.ds((base + (block * 2 + c) * len(group) + group.index(i)) * lanes, lanes)

    def bases_of(p):
        return (0,) if p == 0 else (1, 2)

    def put_left(p, places, c, parts):
        t = jnp.concatenate(parts, axis=0)
        if p == 0:
            rounded = [halves(t)]
        else:
            rounded = split(t)
        step = 2 * probes
        for block, i in places:
            if 0 <= i < rows:
                for n, part in enumerate(rounded):
                    lefts[p][n * step : (n + 1) * step, at_k(block, c, i)] = part

    def left_row(p, c, r):
        put_left(p, ((0, r), (1 + WEST, r + 1), (1 + EAST, r - 1)), c, [b_of(n, c, r) for n in bases_of(p)])

    def put_right(p, block, c, i, one, two):
        step = 2 * probes
        both = one + two
        groups = [jnp.concatenate(both[n : n + 2], axis=0) for n in range(0, len(both), 2)]
        for n, t in enumerate(groups):
            for m, part in zip((n, n + len(groups)), split(t)):
                rights[p][m * step : (m + 1) * step, at_k(block, c, i)] = part

    def tree(terms):
        while len(terms) > 1:
            terms = [terms[n] + terms[n + 1] if n + 1 < len(terms) else terms[n] for n in range(0, len(terms), 2)]
        return terms[0]

    def stencil_row(p, c, i):
        q = quad.at[p, c]

        def row_of(index):
            return q[index, pl.ds(i, 1), :]

        count = 3
        cross = {}
        for d in DIRS:
            for e in range(d, 4):
                cross[d, e] = row_of(count)
                count += 1
        ones, twos, arounds = [[] for _ in range(5)], [[] for _ in range(5)], []
        for n in bases_of(p):
            b0 = b_of(n, c, i)
            n_w, n_0, n_e = (north_of(b_of(n, c, i + d), b_of(n, c, i + d, 1)) for d in (-1, 0, 1))
            s_0, s_e = (south_of(b_of(n, c, i + d), b_of(n, c, i + d, 1)) for d in (0, 1))
            n_2 = lane_roll(jnp.where(lane < 2, b_of(n, c, i, 1), b0), -2)
            around = [b_of(n, c, i - 1), b_of(n, c, i + 1), s_0, n_0]
            far = [b0, b_of(n, c, i + 2), s_e, n_e, n_w, n_2]
            arounds.append(around)
            ones[0].append(row_of(0) * b0)
            twos[0].append(row_of(1) * around[EAST] + row_of(2) * around[NORTH])
            for d in DIRS:
                ones[1 + d].append(tree([cross[d, e] * around[e] for e in range(d, 4)]))
                twos[1 + d].append(tree([row_of(count + 6 * d + j) * far[j] for j in range(6)]))
        for d in (SOUTH, NORTH):
            put_left(p, ((1 + d, i),), c, [around[d] for around in arounds])
        for block in range(5):
            put_right(p, block, c, i, ones[block], twos[block])

    def contract(p, group):
        size = probes * len(bases_of(p))
        results = []
        base = (0 if group is inner else cut) * lanes
        step = 2 * len(group) * lanes
        for at, span in ((base, step), (base + step, 4 * step)):
            both = lax.dot_general(
                lefts[p][:, pl.ds(at, span)], rights[p][:, pl.ds(at, span)], (((1,), (1,)), ((), ())),
                preferred_element_type=jnp.float32,
            )
            both = both[0:size, :] + both[size:, :]
            results.append(both[:, 0 : 2 * size] + both[:, 2 * size :])
        return jnp.concatenate(results, axis=1)

    width = FORMS * probes

    def start_sum(p, tile_rows, packed):
        mine = pl.ds((ix * n_gy + iy) * tile_rows, tile_rows)
        landed[p][mine, :] = packed
        tile_src[p][...] = packed
        return [
            pltpu.make_async_remote_copy(
                src_ref=tile_src[p], dst_ref=landed[p].at[mine], send_sem=ar_send.at[p], recv_sem=ar_recv.at[p],
                device_id=peer, device_id_type=MESH,
            )
            for peer in peers
        ]

    def everyone(p):
        total_rows = pl.ds(0, (PAIR, rows)[p] * len(peers))
        return pltpu.make_async_remote_copy(
            src_ref=landed[p].at[total_rows], dst_ref=landed[p].at[total_rows], send_sem=ar_send.at[p],
            recv_sem=ar_recv.at[p], device_id=peers[0], device_id_type=MESH,
        )

    def start_first(sums):
        grams = widened(sums)
        packed = grams
        for q in range(1, probes // PAIR):
            packed = jnp.where(lane < q * width, packed, lane_roll(sub_roll(grams, -PAIR * q), q * width))
        return start_sum(0, PAIR, packed[0:PAIR, :])

    def start_second(forms):
        for copy in start_sum(1, rows, jnp.concatenate([forms[0:probes, :], forms[probes:, :]], axis=1)):
            copy.start()

    def landed_sum(p):
        return tree([landed[p][k * probes : (k + 1) * probes, :] for k in range(landed[p].shape[0] // probes)])

    def first_grams():
        packed = landed_sum(0)
        shift = PAIR
        while shift < probes:
            packed = packed + sub_roll(packed, shift)
            shift *= 2
        grams = packed
        for q in range(1, probes // PAIR):
            grams = jnp.where(sub < PAIR * q, grams, lane_roll(packed, -q * width))
        stacked = jnp.concatenate([grams[:, f * probes : (f + 1) * probes] for f in range(FORMS)], axis=0)
        pick = (lane == sub).astype(jnp.float32)[:, 0:probes]
        return widened(grams[:, 0:width] + dot(pick, stacked, ((1,), (1,))))

    def widened(t):
        return jnp.concatenate([t, jnp.zeros((probes, lanes - width), jnp.float32)], axis=1)

    def dot(a, b, dims):
        return lax.dot_general(a, b, (dims, ((), ())), precision=HIGHEST, preferred_element_type=jnp.float32)

    def second_grams(mixing):
        forms = landed_sum(1)
        size = 2 * probes
        forms = jnp.concatenate([forms[:, 0 : FORMS * size], forms[:, FORMS * size :]], axis=0)
        half_mixed = dot(mixing, forms, ((1,), (0,)))
        stacked = jnp.concatenate([half_mixed[:, f * size : (f + 1) * size] for f in range(FORMS)], axis=0)
        full = dot(stacked, mixing, ((1,), (1,)))
        parts = [full[f * probes : (f + 1) * probes, :] for f in range(FORMS)]
        return widened(jnp.concatenate(parts, axis=1) + dot(mixing, stacked, ((1,), (1,))))

    def mixing_of(grams):
        diff = grams - lane_roll(grams, -probes)
        upper = jnp.where(lane < 2 * probes, diff, lane_roll(grams, 2 * probes))
        lower = jnp.where(lane < 2 * probes, lane_roll(diff, -probes), lane_roll(grams, probes))
        size = 2 * probes
        both = [upper, lower]
        scale = [jnp.sum(jnp.where(lane == sub + h * probes, both[h], 0.0), axis=1, keepdims=True) for h in range(2)]
        for k in range(size):
            h, r = k // probes, k % probes
            line = both[h][r : r + 1, :]
            pivot = line[:, k : k + 1]
            inv = jnp.where(pivot > 1e-6 * scale[h][r : r + 1, :], 1.0 / pivot, 0.0)
            line = line * inv
            for q in range(2):
                updated = both[q] - both[q][:, k : k + 1] * line
                both[q] = jnp.where(sub == r, line, updated) if q == h else updated
        return jnp.transpose(jnp.concatenate(both, axis=0))[size : size + probes, :]

    prepare(0)
    for r in range(-2, rows + 2):
        h, at = where_row(r)
        main = probes_ref[:, at, :] if h == 0 else hrow[2 * per_tile : 2 * per_tile + probes, at, :]
        side = probe_strip[:, h * rows + at, :]
        for c in range(2):
            d_main, d_side = main_strip(drv, (c,), r)
            bx[0, c, r + 2, 0] = main * d_main
            bx[0, c, r + 2, 1] = side * d_side

    def surface(c, r):
        m, s = b_of(0, c, r), b_of(0, c, r, 1)
        sides = [
            (b_of(0, c, r - 1), b_of(0, c, r - 1, 1)), (b_of(0, c, r + 1), b_of(0, c, r + 1, 1)),
            (south_of(m, s), south_of(s, m)), (north_of(m, s), north_of(s, m)),
        ]
        hs = [main_strip(kept_ref, (0, c, d), r) for d in DIRS]
        return [tree([hs[d][k] * sides[d][k] for d in DIRS]) for k in range(2)]

    sent_rows = (0, 1, rows - 1)
    got_rows = (rows, rows + 1, -1)
    for n, r in enumerate(sent_rows):
        for c in range(2):
            x = surface(c, r)
            for k in range(2):
                edge_src[n, c, k] = x[k]
    for copy, _, has_dst, _ in edges:
        pl.when(has_dst)(copy.start)
    for c in range(2):
        for r in range(-1, rows + 1):
            left_row(0, c, r)
        for i in inner:
            stencil_row(0, c, i)
    sums = contract(0, inner)
    for c in range(2):
        for i in outer:
            stencil_row(0, c, i)
    sums = sums + contract(0, outer)
    for k in range(1, rounds):
        meet(k)
    waiting = start_first(sums)

    def send_one():
        if waiting:
            waiting.pop(0).start()

    prepare(1, send_one)
    while waiting:
        send_one()

    def fill_row(c, r, x):
        g = main_strip(green, (0, c, last), r)
        w = main_strip(wmx, (), r)
        for k in range(2):
            bx[1, c, r + 2, k] = (g[k] * w[k]) * b_of(0, c, r, k)
            bx[2, c, r + 2, k] = w[k] * x[k]

    for c in range(2):
        for r in range(rows):
            fill_row(c, r, [edge_src[sent_rows.index(r), c, k] for k in range(2)] if r in sent_rows else surface(c, r))
    for c in range(2):
        for r in range(rows):
            left_row(1, c, r)
        for i in inner:
            stencil_row(1, c, i)
    for copy, _, _, has_src in edges:
        pl.when(has_src)(copy.wait_recv)
    sums = contract(1, inner)
    for n, r in enumerate(got_rows):
        for c in range(2):
            fill_row(c, r, [edge_dst[n, c, k] for k in range(2)])
    for c in range(2):
        left_row(1, c, -1)
        left_row(1, c, rows)
        for i in outer:
            stencil_row(1, c, i)
    start_second(sums + contract(1, outer))
    for i in range(rows):
        at = pl.ds(i * lanes, lanes)
        for n in bases_of(1):
            total = [None, None]
            for c in range(2):
                drive = drv[c, 0, pl.ds(i, 1), :]
                m, s = b_of(n, c, i), b_of(n, c, i, 1)
                around = [b_of(n, c, i - 1), b_of(n, c, i + 1), south_of(m, s), north_of(m, s)]
                parts = [
                    (drive * green[1, c, 0, 0, pl.ds(i, 1), :]) * m,
                    drive * tree([kept_ref[1, c, d, 0, pl.ds(i, 1), :] * around[d] for d in DIRS]),
                ]
                total = [b if a is None else a + b for a, b in zip(total, parts)]
            for k in range(2):
                results[k, (n - 1) * probes : n * probes, at] = total[k]
    everyone(0).wait_recv()
    mixing = mixing_of(first_grams())
    for k in range(2):
        mixed[k * probes : (k + 1) * probes, :] = dot(mixing, results[k], ((1,), (0,)))
    everyone(1).wait_recv()
    final = dot(mixing_of(second_grams(mixing)), mixed[...], ((1,), (0,)))
    for i in range(rows):
        out_ref[:, i, :] = final[:, i * lanes : (i + 1) * lanes]
    for copy, _, has_dst, _ in exchange + edges:
        pl.when(has_dst)(copy.wait_send)
    for p in range(2):
        everyone(p).wait_send()


def body(sizes, velocity, thickness, log_friction, obs_weight, ice_mask, grounded, probes):
    layers, rows, lanes = velocity.shape[1:]
    count = probes.shape[0]
    n_gx, n_gy = sizes
    fields = 2 * (layers + 1) + count + 2 + 3
    forms = 1 + 2 + 10 + 24

    def vmem(*shape):
        return pltpu.VMEM(shape, jnp.float32)

    def half(*shape):
        return pltpu.VMEM(shape, jnp.bfloat16)

    sem = pltpu.SemaphoreType.DMA
    scratch = [
        vmem(*velocity.shape), vmem(rows, lanes), vmem(rows, lanes), vmem(rows, lanes),
        pltpu.VMEM((rows, lanes), jnp.int32), pltpu.VMEM((rows, lanes), jnp.int32), vmem(*probes.shape),
        vmem(fields, rows, lanes), vmem(fields, rows, lanes), vmem(3, 2 * rows, lanes), vmem(3, 2 * rows, lanes),
        vmem(3, 2, 2, count, lanes), vmem(3, 2, 2, count, lanes),
        vmem(2, 4, layers, 4, rows, lanes), vmem(layers - 1, 4, rows, lanes), vmem(2, layers - 1, 4, rows, lanes),
        vmem(2, layers, 4, rows, lanes), vmem(2, 2, layers, 4, rows, lanes),
        vmem(2, 2, 4, 4, rows, lanes), vmem(2, 2, forms, rows, lanes),
        vmem(2, 4, rows, lanes), vmem(4, rows, lanes), vmem(count, 2 * rows, lanes),
        vmem(3, 2, rows + 4, 2, count, lanes),
        half(2 * count, 10 * rows * lanes), half(4 * count, 10 * rows * lanes),
        half(4 * count, 10 * rows * lanes), half(8 * count, 10 * rows * lanes),
        vmem(2, 2 * count, rows * lanes), vmem(2 * count, rows * lanes),
        vmem(PAIR, lanes), vmem(rows, lanes), vmem(PAIR * n_gx * n_gy, lanes), vmem(rows * n_gx * n_gy, lanes),
        sem((10,)), sem((10,)), sem((2,)), sem((2,)), sem((7,)),
        pltpu.SemaphoreType.REGULAR((max(rounds_of(n_gy), 1),)),
    ]
    return pl.pallas_call(
        functools.partial(kernel, sizes),
        out_shape=pltpu.VMEM(probes.shape, jnp.float32),
        in_specs=[pl.BlockSpec(memory_space=pltpu.HBM)] * 7,
        out_specs=pl.BlockSpec(memory_space=pltpu.VMEM),
        scratch_shapes=scratch,
        compiler_params=pltpu.CompilerParams(collective_id=0, has_side_effects=True),
        name="hessian_probe",
    )(velocity, thickness, log_friction, obs_weight, ice_mask, grounded, probes)


def solution(mesh):
    sizes = (mesh.shape["gx"], mesh.shape["gy"])
    in_specs = (
        P(None, None, "gx", "gy"),
        P("gx", "gy"),
        P("gx", "gy"),
        P("gx", "gy"),
        P("gx", "gy"),
        P("gx", "gy"),
        P(None, "gx", "gy"),
    )
    out_specs = P(None, "gx", "gy")
    return jax.shard_map(
        functools.partial(body, sizes), mesh=mesh, in_specs=in_specs, out_specs=out_specs, check_vma=False
    )
```

```python
import functools

import jax
import jax.numpy as jnp
from jax import lax
from jax.experimental import pallas as pl
from jax.experimental.pallas import tpu as pltpu
from jax.sharding import PartitionSpec as P

MASS_TERM = 0.1
STRAIN_OFFSET = 0.01
ANISO_X = (4.0, 1.0)
ANISO_Y = (1.0, 4.0)
HIGHEST = lax.Precision.HIGHEST
MESH = pl.DeviceIdType.MESH
PAIR = 2
REACH = 5
SLOT = 2 * REACH
WEST, EAST, SOUTH, NORTH = range(4)
DIRS = range(4)
FORMS = 4


def rounds_of(count):
    rounds = 0
    while 2 ** (rounds + 1) < count - 1:
        rounds += 1
    return rounds


class Field:
    def __init__(self, tiles):
        self.tiles = tiles

    def _with(self, other, op):
        if isinstance(other, Field):
            return Field([None if a is None or b is None else op(a, b) for a, b in zip(self.tiles, other.tiles)])
        return Field([None if a is None else op(a, other) for a in self.tiles])

    def __add__(self, other):
        return self._with(other, lambda a, b: a + b)

    def __sub__(self, other):
        return self._with(other, lambda a, b: a - b)

    def __mul__(self, other):
        return self._with(other, lambda a, b: a * b)

    __radd__ = __add__
    __rmul__ = __mul__

    def map(self, op):
        return Field([None if a is None else op(a) for a in self.tiles])


def kernel(
    sizes,
    vel_hbm, thick_hbm, logf_hbm, obs_hbm, ice_hbm, ground_hbm, probes_hbm,
    out_ref,
    vel_ref, thick_ref, logf_ref, obs_ref, ice_ref, ground_ref, probes_ref,
    row, hrow, tn, ts, edge_src, edge_dst,
    coef, kzs, ratio, inverse, green, kept_ref, quad, drv, wmx, probe_strip,
    bx, left_0, right_0, left_1, right_1, results, mixed, tile_0, tile_1, landed_0, landed_1,
    send_sem, recv_sem, ar_send, ar_recv, in_sem, greet_sem,
):
    n_gx, n_gy = sizes
    lefts, rights, tile_src, landed = (left_0, left_1), (right_0, right_1), (tile_0, tile_1), (landed_0, landed_1)
    loads = [
        pltpu.make_async_copy(src, dst, in_sem.at[k])
        for k, (src, dst) in enumerate((
            (vel_hbm, vel_ref), (probes_hbm, probes_ref), (thick_hbm, thick_ref), (logf_hbm, logf_ref),
            (obs_hbm, obs_ref), (ice_hbm, ice_ref), (ground_hbm, ground_ref),
        ))
    ]
    for copy in loads:
        copy.start()
    layers = vel_ref.shape[1]
    rows = vel_ref.shape[2]
    lanes = vel_ref.shape[3]
    probes = probes_ref.shape[0]
    last = layers - 1
    half = rows // 2
    per_tile = layers + 1
    n_fields = 2 * per_tile + probes + 2
    ix = lax.axis_index("gx")
    iy = lax.axis_index("gy")
    tile = (rows, lanes)
    lane = lax.broadcasted_iota(jnp.int32, tile, 1)
    sub = lax.broadcasted_iota(jnp.int32, tile, 0)
    lane_first = lane == 0
    lane_last = lane == lanes - 1
    sub_first = sub == 0
    sub_last = sub == rows - 1
    slot_id = lane // SLOT
    high = lane - slot_id * SLOT < REACH

    barrier = pltpu.get_barrier_semaphore()
    peers = [
        {"gx": lax.rem(ix + step // n_gy, n_gx), "gy": lax.rem(iy + step % n_gy, n_gy)} for step in sorted(range(1, n_gx * n_gy), key=lambda step: -min(step % n_gy, n_gy - step % n_gy))
    ]
    def lane_roll(t, shift):
        shift = shift % lanes
        return t if shift == 0 else pltpu.roll(t, shift, 1)

    def sub_roll(t, shift):
        return pltpu.roll(t, shift % rows, 0)

    def inside(dx, dy):
        tests = []
        if dx:
            tests.append(ix >= -dx if dx < 0 else ix < n_gx - dx)
        if dy:
            tests.append(iy >= -dy if dy < 0 else iy < n_gy - dy)
        return functools.reduce(jnp.logical_and, tests)

    def transfer(k, dx, dy, src, dst):
        target = {}
        if dx:
            target["gx"] = ix + dx
        if dy:
            target["gy"] = iy + dy
        copy = pltpu.make_async_remote_copy(
            src_ref=src, dst_ref=dst, send_sem=send_sem.at[k], recv_sem=recv_sem.at[k],
            device_id=target, device_id_type=MESH,
        )
        return copy, dst, inside(dx, dy), inside(-dx, -dy)

    for dy in (0, -1, 1, -2, 2):
        for step in range(n_gx):
            if step == 0 and dy == 0:
                continue
            target = {"gx": lax.rem(ix + step, n_gx), "gy": iy + dy}
            if dy == 0:
                pl.semaphore_signal(barrier, inc=1, device_id=target, device_id_type=MESH)
            else:
                @pl.when(inside(0, dy))
                def _(target=target):
                    pl.semaphore_signal(barrier, inc=1, device_id=target, device_id_type=MESH)
    low, top = pl.ds(0, half), pl.ds(half, half)
    corner_low, corner_top = pl.ds(rows, half), pl.ds(rows + half, half)
    own_pack = pl.ds(n_fields, 3)
    whole = pl.ds(0, rows)
    everything = pl.ds(0, n_fields + 3)
    packs = pl.ds(0, 3)
    exchange = [
        transfer(0, -1, 0, row.at[everything, low], hrow.at[everything, low]),
        transfer(1, 1, 0, row.at[everything, top], hrow.at[everything, top]),
        transfer(2, 0, -1, row.at[own_pack, whole], tn.at[packs, whole]),
        transfer(3, 0, 1, row.at[own_pack, whole], ts.at[packs, whole]),
        transfer(4, -1, -1, row.at[own_pack, low], tn.at[packs, corner_low]),
        transfer(5, 1, -1, row.at[own_pack, top], tn.at[packs, corner_top]),
        transfer(6, -1, 1, row.at[own_pack, low], ts.at[packs, corner_low]),
        transfer(7, 1, 1, row.at[own_pack, top], ts.at[packs, corner_top]),
    ]
    ahead, behind = pl.ds(0, 2), pl.ds(2, 1)
    edges = [
        transfer(8, -1, 0, edge_src.at[ahead], edge_dst.at[ahead]),
        transfer(9, 1, 0, edge_src.at[behind], edge_dst.at[behind]),
    ]

    for copy in loads:
        copy.wait()
    mask_own = ice_ref[...].astype(jnp.float32)
    friction_own = mask_own * ground_ref[...].astype(jnp.float32) * jnp.exp(logf_ref[...])
    wm_own = obs_ref[...] * mask_own
    own = [vel_ref[0, l] for l in range(layers)] + [thick_ref[...]]
    own += [vel_ref[1, l] for l in range(layers)] + [mask_own]
    own += [probes_ref[p] for p in range(probes)] + [friction_own, wm_own]
    for f, t in enumerate(own):
        row[f] = t
    for k in range(3):
        packed = None
        for s, t in enumerate(own[k * per_tile : (k + 1) * per_tile]):
            moved = lane_roll(t, s * SLOT + REACH)
            packed = moved if packed is None else jnp.where(slot_id == s, moved, packed)
        row[n_fields + k] = packed

    within = sum(inside(0, dy).astype(jnp.int32) for dy in (-1, 1, -2, 2)) + 1
    pl.semaphore_wait(barrier, n_gx * within - 1)
    for copy, _, has_dst, _ in exchange:
        pl.when(has_dst)(copy.start)
    for _, dst, _, has_src in exchange + edges:
        @pl.when(jnp.logical_not(has_src))
        def _(dst=dst):
            dst[...] = jnp.zeros(dst.shape, jnp.float32)

    def greet(k):
        for dy in (-(2 ** (k + 1)), 2 ** (k + 1)):
            @pl.when(inside(0, dy))
            def _(dy=dy):
                pl.semaphore_signal(greet_sem.at[k], inc=1, device_id={"gy": iy + dy}, device_id_type=MESH)

    def meet(k):
        if k < rounds:
            reach = 2 ** (k + 1)
            pl.semaphore_wait(
                greet_sem.at[k], inside(0, -reach).astype(jnp.int32) + inside(0, reach).astype(jnp.int32)
            )
        if k + 1 < rounds:
            greet(k + 1)

    rounds = rounds_of(n_gy)
    if rounds:
        greet(0)
    meet(0)
    for copy, _, _, has_src in exchange:
        pl.when(has_src)(copy.wait_recv)

    def shifted(f, axis, forward):
        if axis == 0:
            at, move, pairs = (sub_first, -1, ((0, 1), (1, 0), (2, 3), (3, 2))) if forward else (sub_last, 1, ((0, 1), (1, 0), (2, 3), (3, 2)))
            roll = sub_roll
        else:
            at, move, pairs = (lane_first, -1, ((0, 2), (1, 3), (2, 0), (3, 1))) if forward else (lane_last, 1, ((0, 2), (1, 3), (2, 0), (3, 1)))
            roll = lane_roll
        tiles = [None] * 4
        for a, b in pairs:
            if f.tiles[a] is not None and f.tiles[b] is not None:
                tiles[a] = roll(jnp.where(at, f.tiles[b], f.tiles[a]), move)
        return Field(tiles)

    def neighbour(f, d):
        return shifted(f, 0 if d in (WEST, EAST) else 1, d in (EAST, NORTH))

    both_packs = [
        [jnp.where(high, ts[k, pl.ds(h * rows, rows), :], tn[k, pl.ds(h * rows, rows), :]) for h in range(2)]
        for k in range(3)
    ]

    def strip(packs_of, s):
        return [lane_roll(t, -(s * SLOT + REACH)) for t in packs_of]

    def assemble(f):
        return Field([own[f], hrow[f]] + strip(both_packs[f // per_tile], f % per_tile))

    thick = assemble(layers).map(lambda t: jnp.where(t > 0.0, t, 1.0))
    inverse_step = thick.map(lambda t: last / t)
    mask = assemble(per_tile + layers)
    friction = assemble(2 * per_tile + probes)
    wm = assemble(2 * per_tile + probes + 1)

    def viscosity(ux, uy, uz, vx, vy, vz):
        shear = uy + vx
        strain = ux * ux + vy * vy + ux * vy + 0.25 * (shear * shear) + 0.25 * (uz * uz + vz * vz) + STRAIN_OFFSET
        root = jnp.exp(jnp.log(strain) * (-1.0 / 3.0))
        root = root + root * (1.0 - strain * root * root * root) * (1.0 / 3.0)
        return 0.5 * root

    strips = []
    for north_side in (True, False):
        def side(k):
            tiles = []
            for h in range(2):
                mine = row[n_fields + k] if h == 0 else hrow[n_fields + k]
                theirs = (tn if north_side else ts)[k, pl.ds(h * rows, rows), :]
                tiles.append(jnp.where(high, mine, theirs) if north_side else jnp.where(high, theirs, mine))
            return tiles
        u_side, v_side = side(0), side(1)
        steps = []
        for t in u_side:
            t = jnp.where(t > 0.0, t, 1.0)
            have = 1
            while have < per_tile:
                t = jnp.where(slot_id >= per_tile - have, t, lane_roll(t, -SLOT * have))
                have *= 2
            steps.append((0.5 * last) / t)
        mu = []
        grads = []
        for pair in (u_side, v_side):
            e = [sub_roll(jnp.where(sub_first, pair[1 - h], pair[h]), -1) for h in range(2)]
            w = [sub_roll(jnp.where(sub_last, pair[1 - h], pair[h]), 1) for h in range(2)]
            for h in range(2):
                t = pair[h]
                n, s = lane_roll(t, -1), lane_roll(t, 1)
                above = jnp.where(slot_id == last, t, lane_roll(t, -SLOT))
                below = jnp.where(slot_id == 0, t, lane_roll(t, SLOT))
                grads.append((0.5 * (e[h] - w[h]), 0.5 * (n - s), (above - below) * steps[h]))
        for h in range(2):
            mu.append(viscosity(*grads[h], *grads[2 + h]))
        strips.append(mu)
    mu_packs = [jnp.where(high, strips[1][h], strips[0][h]) for h in range(2)]

    half_step = Field((0.5 * inverse_step).tiles[:2] + [None, None])
    velocity = []
    for c in range(2):
        for l in range(layers):
            velocity.append(assemble(c * per_tile + l))
    visc = []
    for l in range(layers):
        grads = []
        for c in range(2):
            f = velocity[c * layers + l]
            main = Field(f.tiles[:2] + [None, None])
            gx = 0.5 * (neighbour(main, EAST) - neighbour(main, WEST))
            gy = 0.5 * (neighbour(f, NORTH) - neighbour(f, SOUTH))
            gz = (velocity[c * layers + min(l + 1, last)] - velocity[c * layers + max(l - 1, 0)]) * half_step
            grads.append((gx, gy, gz))
        (ux, uy, uz), (vx, vy, vz) = grads
        tiles = [
            viscosity(ux.tiles[h], uy.tiles[h], uz.tiles[h], vx.tiles[h], vy.tiles[h], vz.tiles[h]) for h in range(2)
        ]
        visc.append(Field(tiles + strip(mu_packs, l)))

    def store(ref, index, f):
        for k, t in enumerate(f.tiles):
            if t is not None:
                ref[index + (k,)] = t

    def load(ref, index, count=4):
        return Field([ref[index + (k,)] if k < count else None for k in range(4)])

    def scale_of(c, d):
        return ANISO_X[c] if d in (WEST, EAST) else ANISO_Y[c]

    for c in range(2):
        store(drv, (c,), friction * velocity[c * layers])
    store(wmx, (), wm)
    for p in range(probes):
        for h, t in enumerate(strip(both_packs[2], p)):
            probe_strip[p, pl.ds(h * rows, rows), :] = t

    mask_e = 0.5 * (mask * neighbour(mask, EAST))
    mask_n = 0.5 * (mask * neighbour(mask, NORTH))
    step2 = 0.5 * (inverse_step * inverse_step * mask)
    diag = MASS_TERM * mask + mask.map(lambda t: 1.0 - t)
    for l in range(layers):
        mu = visc[l]
        k_e = (mu + neighbour(mu, EAST)) * mask_e
        k_n = (mu + neighbour(mu, NORTH)) * mask_n
        for d, f in ((WEST, neighbour(k_e, WEST)), (EAST, k_e), (SOUTH, neighbour(k_n, SOUTH)), (NORTH, k_n)):
            for c in range(2):
                store(coef, (c, d, l), f if scale_of(c, d) == 1.0 else scale_of(c, d) * f)
        if l < last:
            store(kzs, (l,), (mu + visc[l + 1]) * step2)

    for c in range(2):
        ratios, inverses = [], []
        for l in range(layers):
            k = [load(coef, (c, d, l)) for d in DIRS]
            pivot = (k[WEST] + k[EAST]) + (k[SOUTH] + k[NORTH]) + diag
            if l == 0:
                pivot = pivot + friction
            if l > 0:
                below = load(kzs, (l - 1,))
                pivot = pivot + below
            if l < last:
                pivot = pivot + load(kzs, (l,))
            if l > 0:
                pivot = pivot - below * ratios[-1]
            inv = pivot.map(lambda t: 1.0 / t)
            inverses.append(inv)
            store(inverse, (c, l), inv)
            if l < last:
                ratios.append(load(kzs, (l,)) * inv)
                store(ratio, (c, l), ratios[-1])
        up = [inverses[0]]
        for l in range(1, layers):
            up.append(load(kzs, (l - 1,)) * up[-1] * inverses[l])
        from_bottom, from_top = up[last], inverses[last]
        for l in range(last, -1, -1):
            if l < last:
                from_bottom = up[l] + ratios[l] * from_bottom
                from_top = ratios[l] * from_top
            store(green, (0, c, l), from_bottom)
            store(green, (1, c, l), from_top)

    def prepare(p, between=lambda: None):
        src, kept = (0, last) if p == 0 else (last, 0)
        for c in range(2):
            quad[p, c, 0] = 0.5 * green[p, c, src, 0]
            cross = {}
            ys = []
            for l in range(layers):
                g = load(green, (p, c, l))
                inv = load(inverse, (c, l), 3)
                f = [load(coef, (c, d, l), 3) * neighbour(g, d) for d in DIRS]
                if l > 0:
                    below = load(kzs, (l - 1,), 3)
                    f = [f[d] + below * ys[-1][d] for d in DIRS]
                ys.append([f[d] * inv for d in DIRS])
                between()
                for d in DIRS:
                    for e in range(d, 4):
                        term = f[d].tiles[0] * ys[-1][e].tiles[0]
                        cross[d, e] = cross[d, e] + term if l > 0 else term
            at = 3
            for (d, e), term in cross.items():
                quad[p, c, at] = 0.5 * term if d == e else term
                at += 1
            x = ys[last]
            total = [[None] * 6 for _ in DIRS]
            for l in range(last, -1, -1):
                if l < last:
                    r = load(ratio, (c, l), 3)
                    x = [ys[l][d] + r * x[d] for d in DIRS]
                between()
                if l == kept:
                    for d in DIRS:
                        for k in (0, 2):
                            kept_ref[p, c, d, k] = x[d].tiles[k]
                if l == src:
                    quad[p, c, 1] = x[EAST].tiles[0]
                    quad[p, c, 2] = x[NORTH].tiles[0]
                he = [sub_roll(jnp.where(sub_first, x[e].tiles[1], x[e].tiles[0]), -1) for e in DIRS]
                hn = [lane_roll(jnp.where(lane_first, x[e].tiles[2], x[e].tiles[0]), -1) for e in DIRS]
                k_e, k_n = coef[c, EAST, l, 0], coef[c, NORTH, l, 0]
                for d in DIRS:
                    t_e, t_n = k_e * x[d].tiles[0], k_n * x[d].tiles[0]
                    terms = [
                        t_e * he[WEST] + t_n * hn[SOUTH], t_e * he[EAST], t_e * he[SOUTH],
                        t_e * he[NORTH] + t_n * hn[EAST], t_n * hn[WEST], t_n * hn[NORTH],
                    ]
                    total[d] = [v if u is None else u + v for u, v in zip(total[d], terms)]
            for d in DIRS:
                for k in range(6):
                    quad[p, c, at] = total[d][k]
                    at += 1

    def where_row(r):
        return (0, r) if 0 <= r < rows else (1, r % rows)

    def main_strip(ref, index, r):
        h, at = where_row(r)
        return ref[index + (h, pl.ds(at, 1), slice(None))], ref[index + (2 + h, pl.ds(at, 1), slice(None))]

    def north_of(m, s):
        return lane_roll(jnp.where(lane_first, s, m), -1)

    def south_of(m, s):
        return lane_roll(jnp.where(lane_last, s, m), 1)

    def b_of(p, c, r, s=0):
        return bx[p, c, r + 2, s]

    def split(t):
        head = t.astype(jnp.bfloat16)
        return head, (t - head.astype(jnp.float32)).astype(jnp.bfloat16)

    def halves(t):
        return jnp.concatenate([t, t - t.astype(jnp.bfloat16).astype(jnp.float32)], axis=0).astype(jnp.bfloat16)

    inner = list(range(1, rows - 2))
    outer = [i for i in range(rows) if i not in inner]
    cut = 10 * len(inner)

    def at_k(block, c, i):
        group = inner if i in inner else outer
        base = 0 if i in inner else cut
        return pl.ds((base + (block * 2 + c) * len(group) + group.index(i)) * lanes, lanes)

    def bases_of(p):
        return (0,) if p == 0 else (1, 2)

    def put_left(p, places, c, parts):
        t = jnp.concatenate(parts, axis=0)
        if p == 0:
            rounded = [halves(t)]
        else:
            rounded = split(t)
        step = 2 * probes
        for block, i in places:
            if 0 <= i < rows:
                for n, part in enumerate(rounded):
                    lefts[p][n * step : (n + 1) * step, at_k(block, c, i)] = part

    def left_row(p, c, r):
        put_left(p, ((0, r), (1 + WEST, r + 1), (1 + EAST, r - 1)), c, [b_of(n, c, r) for n in bases_of(p)])

    def put_right(p, block, c, i, one, two):
        step = 2 * probes
        both = one + two
        groups = [jnp.concatenate(both[n : n + 2], axis=0) for n in range(0, len(both), 2)]
        for n, t in enumerate(groups):
            for m, part in zip((n, n + len(groups)), split(t)):
                rights[p][m * step : (m + 1) * step, at_k(block, c, i)] = part

    def tree(terms):
        while len(terms) > 1:
            terms = [terms[n] + terms[n + 1] if n + 1 < len(terms) else terms[n] for n in range(0, len(terms), 2)]
        return terms[0]

    def stencil_row(p, c, i):
        q = quad.at[p, c]

        def row_of(index):
            return q[index, pl.ds(i, 1), :]

        count = 3
        cross = {}
        for d in DIRS:
            for e in range(d, 4):
                cross[d, e] = row_of(count)
                count += 1
        ones, twos, arounds = [[] for _ in range(5)], [[] for _ in range(5)], []
        for n in bases_of(p):
            b0 = b_of(n, c, i)
            n_w, n_0, n_e = (north_of(b_of(n, c, i + d), b_of(n, c, i + d, 1)) for d in (-1, 0, 1))
            s_0, s_e = (south_of(b_of(n, c, i + d), b_of(n, c, i + d, 1)) for d in (0, 1))
            n_2 = lane_roll(jnp.where(lane < 2, b_of(n, c, i, 1), b0), -2)
            around = [b_of(n, c, i - 1), b_of(n, c, i + 1), s_0, n_0]
            far = [b0, b_of(n, c, i + 2), s_e, n_e, n_w, n_2]
            arounds.append(around)
            ones[0].append(row_of(0) * b0)
            twos[0].append(row_of(1) * around[EAST] + row_of(2) * around[NORTH])
            for d in DIRS:
                ones[1 + d].append(tree([cross[d, e] * around[e] for e in range(d, 4)]))
                twos[1 + d].append(tree([row_of(count + 6 * d + j) * far[j] for j in range(6)]))
        for d in (SOUTH, NORTH):
            put_left(p, ((1 + d, i),), c, [around[d] for around in arounds])
        for block in range(5):
            put_right(p, block, c, i, ones[block], twos[block])

    def contract(p, group):
        size = probes * len(bases_of(p))
        results = []
        base = (0 if group is inner else cut) * lanes
        step = 2 * len(group) * lanes
        for at, span in ((base, step), (base + step, 4 * step)):
            both = lax.dot_general(
                lefts[p][:, pl.ds(at, span)], rights[p][:, pl.ds(at, span)], (((1,), (1,)), ((), ())),
                preferred_element_type=jnp.float32,
            )
            both = both[0:size, :] + both[size:, :]
            results.append(both[:, 0 : 2 * size] + both[:, 2 * size :])
        return jnp.concatenate(results, axis=1)

    width = FORMS * probes

    def start_sum(p, tile_rows, packed):
        mine = pl.ds((ix * n_gy + iy) * tile_rows, tile_rows)
        landed[p][mine, :] = packed
        tile_src[p][...] = packed
        return [
            pltpu.make_async_remote_copy(
                src_ref=tile_src[p], dst_ref=landed[p].at[mine], send_sem=ar_send.at[p], recv_sem=ar_recv.at[p],
                device_id=peer, device_id_type=MESH,
            )
            for peer in peers
        ]

    def everyone(p):
        total_rows = pl.ds(0, (PAIR, rows)[p] * len(peers))
        return pltpu.make_async_remote_copy(
            src_ref=landed[p].at[total_rows], dst_ref=landed[p].at[total_rows], send_sem=ar_send.at[p],
            recv_sem=ar_recv.at[p], device_id=peers[0], device_id_type=MESH,
        )

    def start_first(sums):
        grams = widened(sums)
        packed = grams
        for q in range(1, probes // PAIR):
            packed = jnp.where(lane < q * width, packed, lane_roll(sub_roll(grams, -PAIR * q), q * width))
        return start_sum(0, PAIR, packed[0:PAIR, :])

    def start_second(forms):
        for copy in start_sum(1, rows, jnp.concatenate([forms[0:probes, :], forms[probes:, :]], axis=1)):
            copy.start()

    def landed_sum(p):
        return tree([landed[p][k * probes : (k + 1) * probes, :] for k in range(landed[p].shape[0] // probes)])

    def first_grams():
        packed = landed_sum(0)
        shift = PAIR
        while shift < probes:
            packed = packed + sub_roll(packed, shift)
            shift *= 2
        grams = packed
        for q in range(1, probes // PAIR):
            grams = jnp.where(sub < PAIR * q, grams, lane_roll(packed, -q * width))
        stacked = jnp.concatenate([grams[:, f * probes : (f + 1) * probes] for f in range(FORMS)], axis=0)
        pick = (lane == sub).astype(jnp.float32)[:, 0:probes]
        return widened(grams[:, 0:width] + dot(pick, stacked, ((1,), (1,))))

    def widened(t):
        return jnp.concatenate([t, jnp.zeros((probes, lanes - width), jnp.float32)], axis=1)

    def dot(a, b, dims):
        return lax.dot_general(a, b, (dims, ((), ())), precision=HIGHEST, preferred_element_type=jnp.float32)

    def second_grams(mixing):
        forms = landed_sum(1)
        size = 2 * probes
        forms = jnp.concatenate([forms[:, 0 : FORMS * size], forms[:, FORMS * size :]], axis=0)
        half_mixed = dot(mixing, forms, ((1,), (0,)))
        stacked = jnp.concatenate([half_mixed[:, f * size : (f + 1) * size] for f in range(FORMS)], axis=0)
        full = dot(stacked, mixing, ((1,), (1,)))
        parts = [full[f * probes : (f + 1) * probes, :] for f in range(FORMS)]
        return widened(jnp.concatenate(parts, axis=1) + dot(mixing, stacked, ((1,), (1,))))

    def mixing_of(grams):
        diff = grams - lane_roll(grams, -probes)
        upper = jnp.where(lane < 2 * probes, diff, lane_roll(grams, 2 * probes))
        lower = jnp.where(lane < 2 * probes, lane_roll(diff, -probes), lane_roll(grams, probes))
        size = 2 * probes
        both = [upper, lower]
        scale = [jnp.sum(jnp.where(lane == sub + h * probes, both[h], 0.0), axis=1, keepdims=True) for h in range(2)]
        for k in range(size):
            h, r = k // probes, k % probes
            line = both[h][r : r + 1, :]
            pivot = line[:, k : k + 1]
            inv = jnp.where(pivot > 1e-6 * scale[h][r : r + 1, :], 1.0 / pivot, 0.0)
            line = line * inv
            for q in range(2):
                updated = both[q] - both[q][:, k : k + 1] * line
                both[q] = jnp.where(sub == r, line, updated) if q == h else updated
        return jnp.transpose(jnp.concatenate(both, axis=0))[size : size + probes, :]

    prepare(0)
    for r in range(-2, rows + 2):
        h, at = where_row(r)
        main = probes_ref[:, at, :] if h == 0 else hrow[2 * per_tile : 2 * per_tile + probes, at, :]
        side = probe_strip[:, h * rows + at, :]
        for c in range(2):
            d_main, d_side = main_strip(drv, (c,), r)
            bx[0, c, r + 2, 0] = main * d_main
            bx[0, c, r + 2, 1] = side * d_side

    def surface(c, r):
        m, s = b_of(0, c, r), b_of(0, c, r, 1)
        sides = [
            (b_of(0, c, r - 1), b_of(0, c, r - 1, 1)), (b_of(0, c, r + 1), b_of(0, c, r + 1, 1)),
            (south_of(m, s), south_of(s, m)), (north_of(m, s), north_of(s, m)),
        ]
        hs = [main_strip(kept_ref, (0, c, d), r) for d in DIRS]
        return [tree([hs[d][k] * sides[d][k] for d in DIRS]) for k in range(2)]

    sent_rows = (0, 1, rows - 1)
    got_rows = (rows, rows + 1, -1)
    for n, r in enumerate(sent_rows):
        for c in range(2):
            x = surface(c, r)
            for k in range(2):
                edge_src[n, c, k] = x[k]
    for copy, _, has_dst, _ in edges:
        pl.when(has_dst)(copy.start)
    for c in range(2):
        for r in range(-1, rows + 1):
            left_row(0, c, r)
        for i in inner:
            stencil_row(0, c, i)
    sums = contract(0, inner)
    for c in range(2):
        for i in outer:
            stencil_row(0, c, i)
    sums = sums + contract(0, outer)
    for k in range(1, rounds):
        meet(k)
    waiting = start_first(sums)

    def send_one():
        if waiting:
            waiting.pop(0).start()

    prepare(1, send_one)
    while waiting:
        send_one()

    def fill_row(c, r, x):
        g = main_strip(green, (0, c, last), r)
        w = main_strip(wmx, (), r)
        for k in range(2):
            bx[1, c, r + 2, k] = (g[k] * w[k]) * b_of(0, c, r, k)
            bx[2, c, r + 2, k] = w[k] * x[k]

    for c in range(2):
        for r in range(rows):
            fill_row(c, r, [edge_src[sent_rows.index(r), c, k] for k in range(2)] if r in sent_rows else surface(c, r))
    for c in range(2):
        for r in range(rows):
            left_row(1, c, r)
        for i in inner:
            stencil_row(1, c, i)
    for copy, _, _, has_src in edges:
        pl.when(has_src)(copy.wait_recv)
    sums = contract(1, inner)
    for n, r in enumerate(got_rows):
        for c in range(2):
            fill_row(c, r, [edge_dst[n, c, k] for k in range(2)])
    for c in range(2):
        left_row(1, c, -1)
        left_row(1, c, rows)
        for i in outer:
            stencil_row(1, c, i)
    start_second(sums + contract(1, outer))
    for i in range(rows):
        at = pl.ds(i * lanes, lanes)
        for n in bases_of(1):
            total = [None, None]
            for c in range(2):
                drive = drv[c, 0, pl.ds(i, 1), :]
                m, s = b_of(n, c, i), b_of(n, c, i, 1)
                around = [b_of(n, c, i - 1), b_of(n, c, i + 1), south_of(m, s), north_of(m, s)]
                parts = [
                    (drive * green[1, c, 0, 0, pl.ds(i, 1), :]) * m,
                    drive * tree([kept_ref[1, c, d, 0, pl.ds(i, 1), :] * around[d] for d in DIRS]),
                ]
                total = [b if a is None else a + b for a, b in zip(total, parts)]
            for k in range(2):
                results[k, (n - 1) * probes : n * probes, at] = total[k]
    everyone(0).wait_recv()
    mixing = mixing_of(first_grams())
    for k in range(2):
        mixed[k * probes : (k + 1) * probes, :] = dot(mixing, results[k], ((1,), (0,)))
    everyone(1).wait_recv()
    final = dot(mixing_of(second_grams(mixing)), mixed[...], ((1,), (0,)))
    for i in range(rows):
        out_ref[:, i, :] = final[:, i * lanes : (i + 1) * lanes]
    for copy, _, has_dst, _ in exchange + edges:
        pl.when(has_dst)(copy.wait_send)
    for p in range(2):
        everyone(p).wait_send()


def body(sizes, velocity, thickness, log_friction, obs_weight, ice_mask, grounded, probes):
    layers, rows, lanes = velocity.shape[1:]
    count = probes.shape[0]
    n_gx, n_gy = sizes
    fields = 2 * (layers + 1) + count + 2 + 3
    forms = 1 + 2 + 10 + 24

    def vmem(*shape):
        return pltpu.VMEM(shape, jnp.float32)

    def half(*shape):
        return pltpu.VMEM(shape, jnp.bfloat16)

    sem = pltpu.SemaphoreType.DMA
    scratch = [
        vmem(*velocity.shape), vmem(rows, lanes), vmem(rows, lanes), vmem(rows, lanes),
        pltpu.VMEM((rows, lanes), jnp.int32), pltpu.VMEM((rows, lanes), jnp.int32), vmem(*probes.shape),
        vmem(fields, rows, lanes), vmem(fields, rows, lanes), vmem(3, 2 * rows, lanes), vmem(3, 2 * rows, lanes),
        vmem(3, 2, 2, count, lanes), vmem(3, 2, 2, count, lanes),
        vmem(2, 4, layers, 4, rows, lanes), vmem(layers - 1, 4, rows, lanes), vmem(2, layers - 1, 4, rows, lanes),
        vmem(2, layers, 4, rows, lanes), vmem(2, 2, layers, 4, rows, lanes),
        vmem(2, 2, 4, 4, rows, lanes), vmem(2, 2, forms, rows, lanes),
        vmem(2, 4, rows, lanes), vmem(4, rows, lanes), vmem(count, 2 * rows, lanes),
        vmem(3, 2, rows + 4, 2, count, lanes),
        half(2 * count, 10 * rows * lanes), half(4 * count, 10 * rows * lanes),
        half(4 * count, 10 * rows * lanes), half(8 * count, 10 * rows * lanes),
        vmem(2, 2 * count, rows * lanes), vmem(2 * count, rows * lanes),
        vmem(PAIR, lanes), vmem(rows, lanes), vmem(PAIR * n_gx * n_gy, lanes), vmem(rows * n_gx * n_gy, lanes),
        sem((10,)), sem((10,)), sem((2,)), sem((2,)), sem((7,)),
        pltpu.SemaphoreType.REGULAR((max(rounds_of(n_gy), 1),)),
    ]
    return pl.pallas_call(
        functools.partial(kernel, sizes),
        out_shape=pltpu.VMEM(probes.shape, jnp.float32),
        in_specs=[pl.BlockSpec(memory_space=pltpu.HBM)] * 7,
        out_specs=pl.BlockSpec(memory_space=pltpu.VMEM),
        scratch_shapes=scratch,
        compiler_params=pltpu.CompilerParams(collective_id=0, has_side_effects=True),
        name="hessian_probe",
    )(velocity, thickness, log_friction, obs_weight, ice_mask, grounded, probes)


def solution(mesh):
    sizes = (mesh.shape["gx"], mesh.shape["gy"])
    in_specs = (
        P(None, None, "gx", "gy"),
        P("gx", "gy"),
        P("gx", "gy"),
        P("gx", "gy"),
        P("gx", "gy"),
        P("gx", "gy"),
        P(None, "gx", "gy"),
    )
    out_specs = P(None, "gx", "gy")
    return jax.shard_map(
        functools.partial(body, sizes), mesh=mesh, in_specs=in_specs, out_specs=out_specs, check_vma=False
    )
```
